256 devices in a mesh: nodes: 64 (over y, z, core), rep: 4 (over x).
Axes of the slice: x: 4, y: 4, z: 8, core: 2. Of those that a mesh axis runs over, the one named last changes fastest.
Arguments:
- queries: bfloat16 [4, 32768, 1024], P('rep', 'nodes'), may hold values from -9 to 9
- keys: bfloat16 [4, 32768, 1024], P('rep', 'nodes'), may hold values from -9 to 9
- values: bfloat16 [4, 32768, 1024], P('rep', 'nodes'), may hold values from -6 to 6
- grad_out: bfloat16 [4, 32768, 1024], P('rep', 'nodes'), may hold values from -16 to 16
- w_out: bfloat16 [1024, 1024], replicated, may hold values from -0.1875 to 0.1875
- cluster_id: int32 [4, 32768], P('rep', 'nodes'), may hold values from 0 to 255, as said below
Outputs:
- grad_queries: bfloat16 [4, 32768, 1024], P('rep', 'nodes')
- grad_keys: bfloat16 [4, 32768, 1024], P('rep', 'nodes')
- grad_values: bfloat16 [4, 32768, 1024], P('rep', 'nodes')
- grad_w_out: float32 [1024, 1024], P('nodes')
The draws below stay inside these ranges and needn't reach their ends.
Inputs may be any that keep to these rules, and one draw needn't show every extreme that they name: `cluster_id`: cluster c of a window is owned by index c // 4 of the nodes axis. The 512 nodes of one device name clusters of every owner, exactly 8 nodes for each owner. Clusters differ in size and may be empty.
All inputs are finite; a program needn't handle non-finite values.
Results may differ from the reference program's by a relative error of at most 0.013.
The reference program's roundings to bfloat16 on the way count: a program that leaves them out, or rounds other values in their place, can miss the bound.
Values may be sent and summed in bfloat16 or wider, within the bound.
No kernel may reach another device: no remote copies, remote signals or barrier semaphores. Data moves between devices by JAX's collectives and lax.ppermute only.
A program may use at most 128 MiB of HBM per device.

```python
import math
import jax
import jax.numpy as jnp
from jax import lax

D = 1024
HEADS = 8
HEAD_DIM = 128
CL_DEV = 4
NODE_DEV = 512
BUCKET = 8
NODES_G = 32768
N_NODES = 64
N_REP = 4


def draw_queries(key, part):
    base_rows = jnp.clip(jax.random.normal(jax.random.fold_in(key, 11), (N_REP, NODE_DEV * N_NODES, D), jnp.float32), -6.0, 6.0)
    return base_rows.astype(jnp.bfloat16)


def draw_keys(key, part):
    base_rows = jnp.clip(jax.random.normal(jax.random.fold_in(key, 12), (N_REP, NODE_DEV * N_NODES, D), jnp.float32), -6.0, 6.0)
    return base_rows.astype(jnp.bfloat16)


def draw_cluster_id(key, part):
    bucket = NODE_DEV // N_NODES

    def window_ids(window_key):
        kept = jax.random.randint(jax.random.fold_in(window_key, 1), (N_NODES,), 1, CL_DEV + 1).astype(jnp.int32)
        kept = kept.at[N_NODES - 1].set(CL_DEV)

        def device_ids(device_rank):
            device_key = jax.random.fold_in(window_key, device_rank + 100)
            slot_order = jax.random.permutation(jax.random.fold_in(device_key, 3), NODE_DEV).astype(jnp.int32)
            owner_of = (slot_order // bucket).astype(jnp.int32)
            raw_sub = jax.random.randint(jax.random.fold_in(device_key, 4), (NODE_DEV,), 0, 1048576).astype(jnp.int32)
            sub_cluster = jnp.remainder(raw_sub, kept[owner_of]).astype(jnp.int32)
            return (owner_of * CL_DEV + sub_cluster).astype(jnp.int32)
        return jax.vmap(device_ids)(jnp.arange(N_NODES, dtype=jnp.int32)).reshape(-1)
    window_keys = jax.vmap(lambda window: jax.random.fold_in(key, window))(jnp.arange(N_REP, dtype=jnp.int32))
    return jax.vmap(window_ids)(window_keys)


def strengthened(values, rng, source, target, shards_of, factor):
    owner, partner = [(jnp.arange(values.shape[position]) // (values.shape[position] // shards_of)).reshape([-1 if axis == position else 1 for axis in range(values.ndim)]) for position in (source, target)]
    chosen = jax.random.permutation(rng, shards_of)[partner]
    strong = (owner == chosen) | (owner == (partner + shards_of // 2) % shards_of)
    return jnp.where(strong, factor * values, values)


def steps_of(stream_key, shape, pieces, smallest, high):
    loudness, own = 1.0, jax.random.fold_in(stream_key, 6)
    for position, parts in pieces:
        draws = jnp.exp(jax.random.uniform(jax.random.fold_in(own, position), (parts,), jnp.float32, smallest / len(pieces), high / len(pieces)))
        loudness = loudness * jnp.repeat(draws, shape[position] // parts).reshape([-1 if axis == position else 1 for axis in range(len(shape))])
    return loudness


def bell_draw(own_key, shape, spread, most, split=(), kind=jnp.bfloat16):
    entries = spread * jax.random.normal(own_key, shape, jnp.float32)
    if split:
        entries = entries * steps_of(own_key, shape, split, -0.22, 0.18)
    return jnp.clip(entries, -most, most).astype(kind)


def heavy_noise(key, dims, scale, bound, pieces, heavy, held_as=jnp.bfloat16):
    values = scale * jax.random.normal(key, dims, jnp.float32)
    if pieces:
        values = values * steps_of(key, dims, pieces, -0.22, 0.18)
    return jnp.clip(strengthened(values, jax.random.fold_in(key, 3), *heavy), -bound, bound).astype(held_as)


def setup_inputs(seed: int = 0) -> dict:
    streams_of = jax.random.split(jax.random.key(seed), 7)
    return {
        "queries": draw_queries(jax.random.fold_in(streams_of[6], 71), 0),
        "keys": draw_keys(jax.random.fold_in(streams_of[6], 71), 0),
        "values": bell_draw(streams_of[2], (N_REP, NODES_G, D), 1.0, 6.0, ((0, 4), (1, 64))),
        "grad_out": heavy_noise(streams_of[3], (N_REP, NODES_G, D), 1.0, 16.0, ((0, 4), (1, 64)), (1, 2, 64, 4.0)),
        "w_out": bell_draw(streams_of[4], (D, D), D ** -0.5, 0.1875),
        "cluster_id": draw_cluster_id(jax.random.fold_in(streams_of[6], 71), 0),
    }


big_negative = -1e+30

def head_grads(query_rows, key_rows, value_rows, grad_rows, tag_rows, score_scale):
    scores = lax.dot_general(query_rows, key_rows, (((1,), (1,)), ((), ())), preferred_element_type=jnp.float32) * score_scale
    allowed = (tag_rows[:, None] == tag_rows[None, :]) & (tag_rows[None, :] > 0)
    scores = jnp.where(allowed, scores, big_negative)
    highest = lax.optimization_barrier(jnp.max(scores, axis=1, keepdims=True))
    weights = jnp.exp(scores - highest)
    softmax_rows = weights / lax.optimization_barrier(jnp.sum(weights, axis=1, keepdims=True))
    softmax_low = softmax_rows.astype(jnp.bfloat16)
    attended = jnp.dot(softmax_low, value_rows, preferred_element_type=jnp.float32).astype(jnp.bfloat16)
    delta_rows = lax.optimization_barrier(jnp.sum(grad_rows.astype(jnp.float32) * attended.astype(jnp.float32), axis=1, keepdims=True))
    grad_softmax = lax.dot_general(grad_rows, value_rows, (((1,), (1,)), ((), ())), preferred_element_type=jnp.float32)
    grad_scores = (softmax_rows * (grad_softmax - delta_rows) * score_scale).astype(jnp.bfloat16)
    grad_query = jnp.dot(grad_scores, key_rows, preferred_element_type=jnp.float32).astype(jnp.bfloat16)
    grad_key = lax.dot_general(grad_scores, query_rows, (((0,), (0,)), ((), ())), preferred_element_type=jnp.float32).astype(jnp.bfloat16)
    grad_value = lax.dot_general(softmax_low, grad_rows, (((0,), (0,)), ((), ())), preferred_element_type=jnp.float32).astype(jnp.bfloat16)
    return (grad_query, grad_key, grad_value, attended)

def all_heads(query_all, key_all, value_all, grad_all, tag_all, score_scale):
    collected = [[], [], [], []]
    for head_index in range(query_all.shape[1]):
        outputs = head_grads(query_all[:, head_index], key_all[:, head_index], value_all[:, head_index], grad_all[:, head_index], tag_all[:, head_index], score_scale)
        for member in range(4):
            collected[member].append(outputs[member])
    return tuple((jnp.stack(pieces_list, axis=1) for pieces_list in collected))

def reference(queries, keys, values, grad_out, w_out, cluster_id):
    buffer_rows = N_NODES * BUCKET
    score_scale = 1.0 / math.sqrt(HEAD_DIM)
    nodes_window = queries.shape[1]
    model_width = queries.shape[2]
    head_shape = (buffer_rows, HEADS, HEAD_DIM)
    grad_attended = jnp.dot(grad_out.reshape(-1, model_width), w_out, preferred_element_type=jnp.float32).astype(jnp.bfloat16).reshape(grad_out.shape)
    results_all = [[], [], [], []]
    weight_total = jnp.zeros((model_width, model_width), jnp.float32)
    for window in range(N_REP):
        owner_ids = (cluster_id[window] // CL_DEV).astype(jnp.int32)
        sub_ids = (cluster_id[window] - owner_ids * CL_DEV).astype(jnp.int32)
        sort_order = jnp.argsort(owner_ids, stable=True).astype(jnp.int32)
        owner_range = jnp.arange(N_NODES, dtype=jnp.int32)
        counts = lax.optimization_barrier(jnp.sum((owner_ids[None, :] == owner_range[:, None]).astype(jnp.int32), axis=1)).astype(jnp.int32)
        starts = (jnp.cumsum(counts) - counts).astype(jnp.int32)

        def sorted_padded(array):
            tail = jnp.zeros((buffer_rows,) + array.shape[1:], array.dtype)
            return jnp.concatenate([array[sort_order], tail], axis=0)
        sorted_sets = [sorted_padded(queries[window]), sorted_padded(keys[window]), sorted_padded(values[window]), sorted_padded(grad_attended[window])]
        sorted_tag = sorted_padded(sub_ids + 1)
        sorted_node = sorted_padded(jnp.arange(nodes_window, dtype=jnp.int32))
        initial = tuple((jnp.zeros((nodes_window + 1, model_width), jnp.bfloat16) for member in range(4)))

        def owner_step(carry, owner):
            first_row = starts[owner]
            live = jnp.arange(buffer_rows, dtype=jnp.int32) < counts[owner]
            blocks = []
            for array in sorted_sets:
                taken = lax.dynamic_slice_in_dim(array, first_row, buffer_rows, 0)
                blocks.append(jnp.where(live[:, None], taken, jnp.zeros_like(taken)).reshape(head_shape))
            tag_line = jnp.where(live, lax.dynamic_slice_in_dim(sorted_tag, first_row, buffer_rows, 0), 0).astype(jnp.int32)
            tag_all = jnp.broadcast_to(tag_line[:, None], (buffer_rows, HEADS))
            target = jnp.where(live, lax.dynamic_slice_in_dim(sorted_node, first_row, buffer_rows, 0), nodes_window).astype(jnp.int32)
            results = all_heads(blocks[0], blocks[1], blocks[2], blocks[3], tag_all, score_scale)
            updated = tuple((held.at[target].set(result.reshape(buffer_rows, model_width)) for held, result in zip(carry, results)))
            return (updated, None)
        final, unused = lax.scan(owner_step, initial, owner_range)
        for member in range(4):
            results_all[member].append(final[member][:nodes_window])
        weight_total = weight_total + lax.dot_general(grad_out[window], final[3][:nodes_window], (((0,), (0,)), ((), ())), preferred_element_type=jnp.float32)
    norm_factor = 1.0 / math.sqrt(N_REP * nodes_window)
    grad_queries = jnp.stack(results_all[0], axis=0)
    grad_keys = jnp.stack(results_all[1], axis=0)
    grad_values = jnp.stack(results_all[2], axis=0)
    return (grad_queries, grad_keys, grad_values, weight_total * norm_factor)
```

```python
import math

import jax
import jax.numpy as jnp
from jax import lax
from jax.experimental import pallas as pl
from jax.experimental.pallas import tpu as pltpu
from jax.sharding import PartitionSpec as P

HEAD_DIM = 128
CL_DEV = 4
UNIT = 256
UNITS_A = 2
LANES = 128
big_negative = -1e30
BF = jnp.bfloat16
F32 = jnp.float32


def mm(a, b, dims):
    return lax.dot_general(a, b, (dims, ((), ())), preferred_element_type=F32)


def nn(a, b):
    return mm(a, b, ((1,), (0,)))


def nt(a, b):
    return mm(a, b, ((1,), (1,)))


def tn(a, b):
    return mm(a, b, ((0,), (0,)))


def column_of(row, rows):
    return jnp.transpose(jnp.broadcast_to(row, (LANES, rows)))[:, :1]


def pack_first(rows, bucket, ids_ref, g_ref, q_ref, k_ref, v_ref, out_ref, pick_ref):
    ids_row = ids_ref[...].astype(F32)
    owner_row = jnp.floor(ids_row * (1.0 / CL_DEV))
    ids_col = column_of(ids_row, rows)
    owner_col = jnp.floor(ids_col * (1.0 / CL_DEV))
    tag_col = ids_col - owner_col * CL_DEV + 1.0
    down = lax.broadcasted_iota(jnp.int32, (rows, rows), 0)
    across = lax.broadcasted_iota(jnp.int32, (rows, rows), 1)
    same = (owner_col == owner_row) & (down < across)
    rank = jnp.sum(jnp.where(same, 1.0, 0.0), axis=0, keepdims=True)
    slot = (owner_row * bucket + rank).astype(jnp.int32)
    pick = jnp.where(down == slot, 1.0, 0.0).astype(BF)
    pick_ref[...] = pick
    width = g_ref.shape[1]
    out_ref[:, :width] = nn(pick, g_ref[...]).astype(BF)
    for u in range(q_ref.shape[1] // UNIT):
        for m, ref in enumerate((q_ref, k_ref, v_ref)):
            base = width + (3 * u + m) * UNIT
            out_ref[:, base : base + UNIT] = nn(pick, ref[:, u * UNIT : (u + 1) * UNIT]).astype(BF)
    base = out_ref.shape[1] - LANES
    tags = jnp.broadcast_to(tag_col, (rows, LANES)).astype(BF)
    out_ref[:, base:] = nn(pick, tags).astype(BF)


def pack_rest(pick_ref, q_ref, k_ref, v_ref, out_ref):
    pick = pick_ref[...]
    for m, ref in enumerate((q_ref, k_ref, v_ref)):
        out_ref[:, m * UNIT : (m + 1) * UNIT] = nn(pick, ref[...]).astype(BF)


def attend(scale, g_ref, tag_ref, w_ref, q_ref, k_ref, v_ref, ret_ref, att_ref, bias_ref):
    rows = g_ref.shape[0]

    @pl.when(pl.program_id(0) == 0)
    def _():
        tags = tag_ref[...].astype(F32)
        same = tags[:, :1] == jnp.transpose(tags)[:1, :]
        bias_ref[...] = jnp.where(same, 0.0, big_negative)

    grad_all = nn(g_ref[...], w_ref[...]).astype(BF)
    for h in range(UNIT // HEAD_DIM):
        cols = slice(h * HEAD_DIM, (h + 1) * HEAD_DIM)
        q, k, v, grad = q_ref[:, cols], k_ref[:, cols], v_ref[:, cols], grad_all[:, cols]
        scores = nt(q, k) * scale + bias_ref[...]
        weights = jnp.exp(scores - jnp.max(scores, axis=1, keepdims=True))
        probs = weights * (1.0 / jnp.sum(weights, axis=1, keepdims=True))
        low = probs.astype(BF)
        attended = nn(low, v).astype(BF)
        delta = jnp.sum(grad.astype(F32) * attended.astype(F32), axis=1, keepdims=True)
        grad_scores = (probs * (nt(grad, v) - delta) * scale).astype(BF)
        att_ref[:, cols] = attended
        for m, part in enumerate((nn(grad_scores, k), tn(grad_scores, q), tn(low, grad))):
            base = m * UNIT + h * HEAD_DIM
            ret_ref[:, base : base + HEAD_DIM] = part.astype(BF)


def unpack(held, back_ref, ret_ref, *refs):
    outs = refs[held:]
    for m, ref in enumerate(outs):
        ref[...] = nn(back_ref[...], ret_ref[:, m * UNIT : (m + 1) * UNIT]).astype(BF)


def cost(flops, nbytes, exps=0):
    return pl.CostEstimate(flops=flops, bytes_accessed=nbytes, transcendentals=exps)


def params():
    return pltpu.CompilerParams(vmem_limit_bytes=48 * 1024 * 1024)


def ring(size, shift):
    return [(i, (i + shift) % size) for i in range(size)]


def local(sizes, queries, keys, values, grad_out, w_out, cluster_id):
    ny, nz, nc, nx = sizes
    node_count = ny * nz * nc
    rows = queries.shape[1]
    width = queries.shape[2]
    bucket = rows // node_count
    units = width // UNIT
    ua, ub = UNITS_A, units - UNITS_A
    scale = 1.0 / math.sqrt(HEAD_DIM)
    norm_factor = 1.0 / math.sqrt(nx * node_count * rows)
    q, k, v, g = queries[0], keys[0], values[0], grad_out[0]

    def sds(shape, dtype=BF):
        return jax.ShapeDtypeStruct(shape, dtype)

    def full(shape):
        return pl.BlockSpec(shape, lambda *_: (0,) * len(shape))

    def exchange(rows_in):
        c = rows_in.shape[1]
        out = lax.all_to_all(
            rows_in.reshape(node_count, bucket, c), "nodes", split_axis=0, concat_axis=0, tiled=True
        )
        return out.reshape(rows, c)

    wide_a = width + 3 * UNIT * ua + LANES
    part_a = pl.BlockSpec((rows, UNIT * ua), lambda i: (0, 0))
    send_a, pick = pl.pallas_call(
        lambda *refs: pack_first(rows, bucket, *refs),
        out_shape=(sds((rows, wide_a)), sds((rows, rows))),
        grid=(1,),
        in_specs=[full((1, rows)), full((rows, width)), part_a, part_a, part_a],
        out_specs=(full((rows, wide_a)), full((rows, rows))),
        compiler_params=params(),
        cost_estimate=cost(2 * rows * rows * wide_a, 4 * rows * wide_a),
        name="pack_first",
    )(cluster_id, g, q, k, v)
    recv_a = exchange(send_a)

    part_b = pl.BlockSpec((rows, UNIT), lambda i: (0, i + ua))
    send_b = pl.pallas_call(
        pack_rest,
        out_shape=sds((rows, 3 * UNIT * ub)),
        grid=(ub,),
        in_specs=[full((rows, rows)), part_b, part_b, part_b],
        out_specs=pl.BlockSpec((rows, 3 * UNIT), lambda i: (0, i)),
        compiler_params=params(),
        cost_estimate=cost(2 * rows * rows * 3 * UNIT * ub, 4 * rows * 3 * UNIT * ub),
        name="pack_rest",
    )(pick, q, k, v)
    recv_b = exchange(send_b)
    back = jnp.transpose(pick)

    def attention(recv, first, unit0, n_units):
        def col(m):
            return pl.BlockSpec((rows, UNIT), lambda i: (0, first + 3 * i + m))

        return pl.pallas_call(
            lambda *refs: attend(scale, *refs),
            out_shape=(sds((rows, 3 * UNIT * n_units)), sds((rows, UNIT * n_units))),
            grid=(n_units,),
            in_specs=[
                full((rows, width)),
                pl.BlockSpec((rows, LANES), lambda i: (0, wide_a // LANES - 1)),
                pl.BlockSpec((width, UNIT), lambda i: (0, i + unit0)),
                col(0),
                col(1),
                col(2),
            ],
            out_specs=(
                pl.BlockSpec((rows, 3 * UNIT), lambda i: (0, i)),
                pl.BlockSpec((rows, UNIT), lambda i: (0, i)),
            ),
            scratch_shapes=[pltpu.VMEM((rows, rows), F32)],
            compiler_params=params(),
            cost_estimate=cost(
                2 * rows * UNIT * n_units * (6 * rows + width),
                2 * rows * UNIT * n_units * 7 + 4 * rows * width,
                rows * rows * n_units * UNIT // HEAD_DIM,
            ),
            name="attend",
        )(recv_a, recv_a, w_out, recv, recv, recv)

    ret_a, att_a = attention(recv_a, width // UNIT, 0, ua)
    home_a = exchange(ret_a)
    ret_b, att_b = attention(recv_b, 0, ua, ub)
    home_b = exchange(ret_b)

    out_sds = (sds((rows, width)),) * 3
    outs = pl.pallas_call(
        lambda *refs: unpack(0, *refs),
        out_shape=out_sds,
        grid=(ua,),
        in_specs=[full((rows, rows)), pl.BlockSpec((rows, 3 * UNIT), lambda i: (0, i))],
        out_specs=(pl.BlockSpec((rows, UNIT), lambda i: (0, i)),) * 3,
        compiler_params=params(),
        cost_estimate=cost(2 * rows * rows * 3 * UNIT * ua, 4 * rows * 3 * UNIT * ua),
        name="unpack_a",
    )(back, home_a)
    outs = pl.pallas_call(
        lambda *refs: unpack(3, *refs),
        out_shape=out_sds,
        grid=(ub,),
        in_specs=[full((rows, rows)), pl.BlockSpec((rows, 3 * UNIT), lambda i: (0, i))]
        + [pl.BlockSpec(memory_space=pl.ANY)] * 3,
        out_specs=(pl.BlockSpec((rows, UNIT), lambda i: (0, i + ua)),) * 3,
        input_output_aliases={2: 0, 3: 1, 4: 2},
        compiler_params=params(),
        cost_estimate=cost(2 * rows * rows * 3 * UNIT * ub, 4 * rows * 3 * UNIT * ub),
        name="unpack_b",
    )(back, home_b, *outs)

    node = lax.axis_index("nodes")
    ix = lax.axis_index("rep")
    iy, iz, ic = node // (nz * nc), (node // nc) % nz, node % nc

    def nid(y, z, c):
        return ((y % ny) * nz + z % nz) * nc + c % nc

    everyone = [(y, z, c) for y in range(ny) for z in range(nz) for c in range(nc)]

    def hop(dy, dz, dc):
        return [(nid(y, z, c), nid(y + dy, z + dz, c + dc)) for y, z, c in everyone]

    def pick_of(array, index, axis):
        return lax.dynamic_index_in_dim(array, index, axis, keepdims=False)

    att = jnp.concatenate([att_a, att_b], axis=1)
    weight = tn(recv_a[:, :width], att)
    weight = weight.reshape(ny * nz, nc, width // node_count, width)
    total = pick_of(weight, ic, 1)
    for s in range(1, nc):
        sent = pick_of(weight, (ic + s) % nc, 1).astype(BF)
        total = total + lax.ppermute(sent, "nodes", hop(0, 0, s))
    share = width // nx
    weight = total.reshape(width // nc, width)
    total = lax.dynamic_slice_in_dim(weight, ix * share, share, 1)
    for s in range(1, nx):
        sent = lax.dynamic_slice_in_dim(weight, ((ix + s) % nx) * share, share, 1).astype(BF)
        total = total + lax.ppermute(sent, "rep", ring(nx, s))
    weight = total.reshape(ny, width // nc // ny, share)
    total = pick_of(weight, iy, 0)
    for s in range(1, ny):
        sent = pick_of(weight, (iy + s) % ny, 0).astype(BF)
        total = total + lax.ppermute(sent, "nodes", hop(s, 0, 0))
    weight = total.reshape(nz, width // node_count, share)
    total = pick_of(weight, iz, 0)
    for s in range(1, nz):
        sent = pick_of(weight, (iz + s) % nz, 0).astype(BF)
        total = total + lax.ppermute(sent, "nodes", hop(0, s, 0))
    total = total * norm_factor
    grad_weight = jnp.zeros((width // node_count, width), F32)
    grad_weight = lax.dynamic_update_slice_in_dim(grad_weight, total, ix * share, 1)
    low = total.astype(BF)
    for s in range(1, nx):
        came = lax.ppermute(low, "rep", ring(nx, s)).astype(F32)
        at = ((ix + nx - s) % nx) * share
        grad_weight = lax.dynamic_update_slice_in_dim(grad_weight, came, at, 1)
    return (outs[0][None], outs[1][None], outs[2][None], grad_weight)


def solution(mesh):
    nodes, nx = mesh.shape["nodes"], mesh.shape["rep"]
    nc = 2
    nz = 8
    ny = nodes // (nz * nc)
    in_specs = (
        P("rep", "nodes", None),
        P("rep", "nodes", None),
        P("rep", "nodes", None),
        P("rep", "nodes", None),
        P(),
        P("rep", "nodes"),
    )
    out_specs = (
        P("rep", "nodes", None),
        P("rep", "nodes", None),
        P("rep", "nodes", None),
        P("nodes", None),
    )

    def body(*args):
        return local((ny, nz, nc, nx), *args)

    return jax.shard_map(
        body, mesh=mesh, in_specs=in_specs, out_specs=out_specs, check_vma=False
    )
```

```python
import math

import jax
import jax.numpy as jnp
from jax import lax
from jax.experimental import pallas as pl
from jax.experimental.pallas import tpu as pltpu
from jax.sharding import PartitionSpec as P


HEAD_DIM = 128
CL_DEV = 4
UNIT = 256
UNITS_A = 2
LANES = 128
big_negative = -1e30
BF = jnp.bfloat16
F32 = jnp.float32


def mm(a, b, dims):
    return lax.dot_general(a, b, (dims, ((), ())), preferred_element_type=F32)


def nn(a, b):
    return mm(a, b, ((1,), (0,)))


def nt(a, b):
    return mm(a, b, ((1,), (1,)))


def tn(a, b):
    return mm(a, b, ((0,), (0,)))


def column_of(row, rows):
    return jnp.transpose(jnp.broadcast_to(row, (LANES, rows)))[:, :1]


def pack_first(rows, bucket, ids_ref, g_ref, q_ref, k_ref, v_ref, out_ref, pick_ref):
    ids_row = ids_ref[...].astype(F32)
    owner_row = jnp.floor(ids_row * (1.0 / CL_DEV))
    ids_col = column_of(ids_row, rows)
    owner_col = jnp.floor(ids_col * (1.0 / CL_DEV))
    tag_col = ids_col - owner_col * CL_DEV + 1.0
    down = lax.broadcasted_iota(jnp.int32, (rows, rows), 0)
    across = lax.broadcasted_iota(jnp.int32, (rows, rows), 1)
    same = (owner_col == owner_row) & (down < across)
    rank = jnp.sum(jnp.where(same, 1.0, 0.0), axis=0, keepdims=True)
    slot = (owner_row * bucket + rank).astype(jnp.int32)
    pick = jnp.where(down == slot, 1.0, 0.0).astype(BF)
    pick_ref[...] = pick
    width = g_ref.shape[1]
    out_ref[:, :width] = nn(pick, g_ref[...]).astype(BF)
    for u in range(q_ref.shape[1] // UNIT):
        for m, ref in enumerate((q_ref, k_ref, v_ref)):
            base = width + (3 * u + m) * UNIT
            out_ref[:, base : base + UNIT] = nn(pick, ref[:, u * UNIT : (u + 1) * UNIT]).astype(BF)
    base = out_ref.shape[1] - LANES
    tags = jnp.broadcast_to(tag_col, (rows, LANES)).astype(BF)
    out_ref[:, base:] = nn(pick, tags).astype(BF)


def pack_rest(pick_ref, q_ref, k_ref, v_ref, out_ref):
    pick = pick_ref[...]
    for m, ref in enumerate((q_ref, k_ref, v_ref)):
        out_ref[:, m * UNIT : (m + 1) * UNIT] = nn(pick, ref[...]).astype(BF)


def attend(scale, g_ref, tag_ref, w_ref, q_ref, k_ref, v_ref, ret_ref, att_ref, bias_ref):
    @pl.when(pl.program_id(0) == 0)
    def _():
        tags = tag_ref[...].astype(F32)
        same = tags[:, :1] == jnp.transpose(tags)[:1, :]
        bias_ref[...] = jnp.where(same, 0.0, big_negative)

    grad_all = nn(g_ref[...], w_ref[...]).astype(BF)
    for h in range(UNIT // HEAD_DIM):
        cols = slice(h * HEAD_DIM, (h + 1) * HEAD_DIM)
        q, k, v, grad = q_ref[:, cols], k_ref[:, cols], v_ref[:, cols], grad_all[:, cols]
        scores = nt(q, k) * scale + bias_ref[...]
        weights = jnp.exp(scores - jnp.max(scores, axis=1, keepdims=True))
        probs = weights * (1.0 / jnp.sum(weights, axis=1, keepdims=True))
        low = probs.astype(BF)
        attended = nn(low, v).astype(BF)
        delta = jnp.sum(grad.astype(F32) * attended.astype(F32), axis=1, keepdims=True)
        grad_scores = (probs * (nt(grad, v) - delta) * scale).astype(BF)
        att_ref[:, cols] = attended
        for m, part in enumerate((nn(grad_scores, k), tn(grad_scores, q), tn(low, grad))):
            base = m * UNIT + h * HEAD_DIM
            ret_ref[:, base : base + HEAD_DIM] = part.astype(BF)


def unpack(held, back_ref, ret_ref, *refs):
    outs = refs[held:]
    for m, ref in enumerate(outs):
        ref[...] = nn(back_ref[...], ret_ref[:, m * UNIT : (m + 1) * UNIT]).astype(BF)


def spread(nx, at_ref, *refs):
    ins, out_ref = refs[:nx], refs[nx]
    half = ins[0].shape[1] // 2
    for s, ref in enumerate(ins):
        source = lax.rem(at_ref[0] + s, nx)
        for m in range(2):
            cols = pl.ds(pl.multiple_of((m * nx + source) * half, half), half)
            out_ref[:, cols] = ref[:, m * half : (m + 1) * half].astype(F32)


def cost(flops, nbytes, exps=0):
    return pl.CostEstimate(flops=flops, bytes_accessed=nbytes, transcendentals=exps)


def params():
    return pltpu.CompilerParams(vmem_limit_bytes=67043328)


def ring(size, shift):
    return [(i, (i + shift) % size) for i in range(size)]


def local(sizes, queries, keys, values, grad_out, w_out, cluster_id):
    ny, nz, nc, nx = sizes
    node_count = ny * nz * nc
    rows = queries.shape[1]
    width = queries.shape[2]
    bucket = rows // node_count
    units = width // UNIT
    ua, ub = UNITS_A, units - UNITS_A
    scale = 1.0 / math.sqrt(HEAD_DIM)
    norm_factor = 1.0 / math.sqrt(nx * node_count * rows)
    q, k, v, g = queries[0], keys[0], values[0], grad_out[0]

    def sds(shape, dtype=BF):
        return jax.ShapeDtypeStruct(shape, dtype)

    def full(shape):
        return pl.BlockSpec(shape, lambda *_: (0,) * len(shape))

    def exchange(rows_in):
        c = rows_in.shape[1]
        out = lax.all_to_all(
            rows_in.reshape(node_count, bucket, c),
            "nodes",
            split_axis=0,
            concat_axis=0,
            tiled=True,
        )
        return out.reshape(rows, c)

    wide_a = width + 3 * UNIT * ua + LANES
    part_a = pl.BlockSpec((rows, UNIT * ua), lambda i: (0, 0))
    send_a, pick = pl.pallas_call(
        lambda *refs: pack_first(rows, bucket, *refs),
        out_shape=(sds((rows, wide_a)), sds((rows, rows))),
        grid=(1,),
        in_specs=[full((1, rows)), full((rows, width)), part_a, part_a, part_a],
        out_specs=(full((rows, wide_a)), full((rows, rows))),
        compiler_params=params(),
        cost_estimate=cost(2 * rows * rows * wide_a, 4 * rows * wide_a),
        name="pack_first",
    )(cluster_id, g, q, k, v)
    recv_a = exchange(send_a)

    part_b = pl.BlockSpec((rows, UNIT), lambda i: (0, i + ua))
    send_b = pl.pallas_call(
        pack_rest,
        out_shape=sds((rows, 3 * UNIT * ub)),
        grid=(ub,),
        in_specs=[full((rows, rows)), part_b, part_b, part_b],
        out_specs=pl.BlockSpec((rows, 3 * UNIT), lambda i: (0, i)),
        compiler_params=params(),
        cost_estimate=cost(2 * rows * rows * 3 * UNIT * ub, 4 * rows * 3 * UNIT * ub),
        name="pack_rest",
    )(pick, q, k, v)
    recv_b = exchange(send_b)
    back = jnp.transpose(pick)

    def attention(recv, first, unit0, n_units):
        def col(m):
            return pl.BlockSpec((rows, UNIT), lambda i: (0, first + 3 * i + m))

        return pl.pallas_call(
            lambda *refs: attend(scale, *refs),
            out_shape=(sds((rows, 3 * UNIT * n_units)), sds((rows, UNIT * n_units))),
            grid=(n_units,),
            in_specs=[
                full((rows, width)),
                pl.BlockSpec((rows, LANES), lambda i: (0, wide_a // LANES - 1)),
                pl.BlockSpec((width, UNIT), lambda i: (0, i + unit0)),
                col(0),
                col(1),
                col(2),
            ],
            out_specs=(
                pl.BlockSpec((rows, 3 * UNIT), lambda i: (0, i)),
                pl.BlockSpec((rows, UNIT), lambda i: (0, i)),
            ),
            scratch_shapes=[pltpu.VMEM((rows, rows), F32)],
            compiler_params=params(),
            cost_estimate=cost(
                2 * rows * UNIT * n_units * (6 * rows + width),
                2 * rows * UNIT * n_units * 7 + 4 * rows * width,
                rows * rows * n_units * UNIT // HEAD_DIM,
            ),
            name="attend",
        )(recv_a, recv_a, w_out, recv, recv, recv)

    ret_a, att_a = attention(recv_a, width // UNIT, 0, ua)
    home_a = exchange(ret_a)
    ret_b, att_b = attention(recv_b, 0, ua, ub)
    home_b = exchange(ret_b)

    out_sds = (sds((rows, width)),) * 3
    outs = pl.pallas_call(
        lambda *refs: unpack(0, *refs),
        out_shape=out_sds,
        grid=(ua,),
        in_specs=[full((rows, rows)), pl.BlockSpec((rows, 3 * UNIT), lambda i: (0, i))],
        out_specs=(pl.BlockSpec((rows, UNIT), lambda i: (0, i)),) * 3,
        compiler_params=params(),
        cost_estimate=cost(2 * rows * rows * 3 * UNIT * ua, 4 * rows * 3 * UNIT * ua),
        name="unpack_a",
    )(back, home_a)
    outs = pl.pallas_call(
        lambda *refs: unpack(3, *refs),
        out_shape=out_sds,
        grid=(ub,),
        in_specs=[full((rows, rows)), pl.BlockSpec((rows, 3 * UNIT), lambda i: (0, i))]
        + [pl.BlockSpec(memory_space=pl.ANY)] * 3,
        out_specs=(pl.BlockSpec((rows, UNIT), lambda i: (0, i + ua)),) * 3,
        input_output_aliases={2: 0, 3: 1, 4: 2},
        compiler_params=params(),
        cost_estimate=cost(2 * rows * rows * 3 * UNIT * ub, 4 * rows * 3 * UNIT * ub),
        name="unpack_b",
    )(back, home_b, *outs)

    node = lax.axis_index("nodes")
    ix = lax.axis_index("rep")
    iy, iz, ic = node // (nz * nc), (node // nc) % nz, node % nc

    def nid(y, z, c):
        return ((y % ny) * nz + z % nz) * nc + c % nc

    everyone = [(y, z, c) for y in range(ny) for z in range(nz) for c in range(nc)]

    def hop(dy, dz, dc):
        return [(nid(y, z, c), nid(y + dy, z + dz, c + dc)) for y, z, c in everyone]

    def pick_of(array, index, axis):
        return lax.dynamic_index_in_dim(array, index, axis, keepdims=False)

    share = width // nx

    def reduced_over_chip_and_x(att):
        part = att.shape[1] // nx
        weight = tn(recv_a[:, :width], att)
        weight = weight.reshape(ny * nz, nc, width // node_count, att.shape[1])
        total = pick_of(weight, ic, 1)
        for s in range(1, nc):
            sent = pick_of(weight, (ic + s) % nc, 1).astype(BF)
            total = total + lax.ppermute(sent, "nodes", hop(0, 0, s))
        weight = total.reshape(width // nc, att.shape[1])
        came = []
        for s in range(1, nx):
            sent = lax.dynamic_slice_in_dim(weight, ((ix + s) % nx) * part, part, 1).astype(BF)
            came.append(lax.ppermute(sent, "rep", ring(nx, s)))
        total = lax.dynamic_slice_in_dim(weight, ix * part, part, 1)
        for piece in came:
            total = total + piece
        return lax.optimization_barrier(total)

    total_a = reduced_over_chip_and_x(att_a)
    att_b, total_a = lax.optimization_barrier((att_b, total_a))
    weight = jnp.concatenate([total_a, reduced_over_chip_and_x(att_b)], axis=1)
    weight = weight.reshape(ny, width // nc // ny, share)
    came = []
    for s in range(1, ny):
        sent = pick_of(weight, (iy + s) % ny, 0).astype(BF)
        came.append(lax.ppermute(sent, "nodes", hop(s, 0, 0)))
    total = pick_of(weight, iy, 0)
    for piece in came:
        total = total + piece
    total = lax.optimization_barrier(total)
    weight = total.reshape(nz, width // node_count, share)
    came = []
    for s in range(1, nz):
        sent = pick_of(weight, (iz + s) % nz, 0).astype(BF)
        came.append(lax.ppermute(sent, "nodes", hop(0, s, 0)))
    total = pick_of(weight, iz, 0)
    for piece in came:
        total = total + piece
    low = (total * norm_factor).astype(BF)
    pieces = [low] + [lax.ppermute(low, "rep", ring(nx, nx - s)) for s in range(1, nx)]
    grad_weight = pl.pallas_call(
        lambda *refs: spread(nx, *refs),
        out_shape=sds((width // node_count, width), F32),
        in_specs=[pl.BlockSpec(memory_space=pltpu.SMEM)]
        + [pl.BlockSpec(memory_space=pltpu.VMEM)] * nx,
        cost_estimate=cost(0, 6 * width // node_count * width),
        name="spread",
    )(ix.reshape(1), *pieces)
    return (outs[0][None], outs[1][None], outs[2][None], grad_weight)


def solution(mesh):
    nodes, nx = mesh.shape["nodes"], mesh.shape["rep"]
    nc = 2
    nz = 8
    ny = nodes // (nz * nc)
    in_specs = (
        P("rep", "nodes", None),
        P("rep", "nodes", None),
        P("rep", "nodes", None),
        P("rep", "nodes", None),
        P(),
        P("rep", "nodes"),
    )
    out_specs = (
        P("rep", "nodes", None),
        P("rep", "nodes", None),
        P("rep", "nodes", None),
        P("nodes", None),
    )

    def body(*args):
        return local((ny, nz, nc, nx), *args)

    return jax.shard_map(
        body, mesh=mesh, in_specs=in_specs, out_specs=out_specs, check_vma=False
    )
```

```python
import math

import jax
import jax.numpy as jnp
from jax import lax
from jax.experimental import pallas as pl
from jax.experimental.pallas import tpu as pltpu
from jax.sharding import PartitionSpec as P


HEAD_DIM = 128
CL_DEV = 4
UNIT = 256
UNITS_A = 2
LANES = 128
big_negative = -1e30
BF = jnp.bfloat16
F32 = jnp.float32


def mm(a, b, dims):
    return lax.dot_general(a, b, (dims, ((), ())), preferred_element_type=F32)


def nn(a, b):
    return mm(a, b, ((1,), (0,)))


def nt(a, b):
    return mm(a, b, ((1,), (1,)))


def tn(a, b):
    return mm(a, b, ((0,), (0,)))


def column_of(row, rows):
    return jnp.transpose(jnp.broadcast_to(row, (LANES, rows)))[:, :1]


def pack_first(rows, bucket, ids_ref, g_ref, q_ref, k_ref, v_ref, out_ref, pick_ref):
    ids_row = ids_ref[...].astype(F32)
    owner_row = jnp.floor(ids_row * (1.0 / CL_DEV))
    ids_col = column_of(ids_row, rows)
    owner_col = jnp.floor(ids_col * (1.0 / CL_DEV))
    tag_col = ids_col - owner_col * CL_DEV + 1.0
    down = lax.broadcasted_iota(jnp.int32, (rows, rows), 0)
    across = lax.broadcasted_iota(jnp.int32, (rows, rows), 1)
    same = (owner_col == owner_row) & (down < across)
    rank = jnp.sum(jnp.where(same, 1.0, 0.0), axis=0, keepdims=True)
    slot = (owner_row * bucket + rank).astype(jnp.int32)
    pick = jnp.where(down == slot, 1.0, 0.0).astype(BF)
    pick_ref[...] = pick
    width = g_ref.shape[1]
    out_ref[:, :width] = nn(pick, g_ref[...]).astype(BF)
    for u in range(q_ref.shape[1] // UNIT):
        for m, ref in enumerate((q_ref, k_ref, v_ref)):
            base = width + (3 * u + m) * UNIT
            out_ref[:, base : base + UNIT] = nn(pick, ref[:, u * UNIT : (u + 1) * UNIT]).astype(BF)
    base = out_ref.shape[1] - LANES
    tags = jnp.broadcast_to(tag_col, (rows, LANES)).astype(BF)
    out_ref[:, base:] = nn(pick, tags).astype(BF)


def pack_rest(pick_ref, q_ref, k_ref, v_ref, out_ref):
    pick = pick_ref[...]
    for m, ref in enumerate((q_ref, k_ref, v_ref)):
        out_ref[:, m * UNIT : (m + 1) * UNIT] = nn(pick, ref[...]).astype(BF)


def attend(scale, g_ref, tag_ref, w_ref, q_ref, k_ref, v_ref, ret_ref, att_ref, bias_ref):
    @pl.when(pl.program_id(0) == 0)
    def _():
        tags = tag_ref[...].astype(F32)
        same = tags[:, :1] == jnp.transpose(tags)[:1, :]
        bias_ref[...] = jnp.where(same, 0.0, big_negative)

    grad_all = nn(g_ref[...], w_ref[...]).astype(BF)
    for h in range(UNIT // HEAD_DIM):
        cols = slice(h * HEAD_DIM, (h + 1) * HEAD_DIM)
        q, k, v, grad = q_ref[:, cols], k_ref[:, cols], v_ref[:, cols], grad_all[:, cols]
        scores = nt(q, k) * scale + bias_ref[...]
        weights = jnp.exp(scores - jnp.max(scores, axis=1, keepdims=True))
        probs = weights * (1.0 / jnp.sum(weights, axis=1, keepdims=True))
        low = probs.astype(BF)
        attended = nn(low, v).astype(BF)
        delta = jnp.sum(grad.astype(F32) * attended.astype(F32), axis=1, keepdims=True)
        grad_scores = (probs * (nt(grad, v) - delta) * scale).astype(BF)
        att_ref[:, cols] = attended
        for m, part in enumerate((nn(grad_scores, k), tn(grad_scores, q), tn(low, grad))):
            base = m * UNIT + h * HEAD_DIM
            ret_ref[:, base : base + HEAD_DIM] = part.astype(BF)


def unpack(held, back_ref, ret_ref, *refs):
    outs = refs[held:]
    for m, ref in enumerate(outs):
        ref[...] = nn(back_ref[...], ret_ref[:, m * UNIT : (m + 1) * UNIT]).astype(BF)


def finish(factor, nx, at_ref, *refs):
    ins, out_ref = refs[:-1], refs[-1]
    total = ins[0][...].astype(F32)
    for ref in ins[1:]:
        total = total + ref[...].astype(F32)
    total = total * factor
    half = total.shape[1] // nx // 2
    for s in range(nx):
        source = lax.rem(at_ref[0] + s, nx)
        for m in range(2):
            cols = pl.ds(pl.multiple_of((m * nx + source) * half, half), half)
            base = (2 * s + m) * half
            out_ref[:, cols] = total[:, base : base + half]


def cost(flops, nbytes, exps=0):
    return pl.CostEstimate(flops=flops, bytes_accessed=nbytes, transcendentals=exps)


def params():
    return pltpu.CompilerParams(vmem_limit_bytes=67043328)


def ring(size, shift):
    return [(i, (i + shift) % size) for i in range(size)]


def local(sizes, queries, keys, values, grad_out, w_out, cluster_id):
    ny, nz, nc, nx = sizes
    node_count = ny * nz * nc
    rows = queries.shape[1]
    width = queries.shape[2]
    bucket = rows // node_count
    units = width // UNIT
    ua, ub = UNITS_A, units - UNITS_A
    scale = 1.0 / math.sqrt(HEAD_DIM)
    norm_factor = 1.0 / math.sqrt(nx * node_count * rows)
    q, k, v, g = queries[0], keys[0], values[0], grad_out[0]

    def sds(shape, dtype=BF):
        return jax.ShapeDtypeStruct(shape, dtype)

    def full(shape):
        return pl.BlockSpec(shape, lambda *_: (0,) * len(shape))

    def exchange(rows_in):
        c = rows_in.shape[1]
        out = lax.all_to_all(
            rows_in.reshape(node_count, bucket, c),
            "nodes",
            split_axis=0,
            concat_axis=0,
            tiled=True,
        )
        return out.reshape(rows, c)

    wide_a = width + 3 * UNIT * ua + LANES
    part_a = pl.BlockSpec((rows, UNIT * ua), lambda i: (0, 0))
    send_a, pick = pl.pallas_call(
        lambda *refs: pack_first(rows, bucket, *refs),
        out_shape=(sds((rows, wide_a)), sds((rows, rows))),
        grid=(1,),
        in_specs=[full((1, rows)), full((rows, width)), part_a, part_a, part_a],
        out_specs=(full((rows, wide_a)), full((rows, rows))),
        compiler_params=params(),
        cost_estimate=cost(2 * rows * rows * wide_a, 4 * rows * wide_a),
        name="pack_first",
    )(cluster_id, g, q, k, v)
    recv_a = exchange(send_a)

    part_b = pl.BlockSpec((rows, UNIT), lambda i: (0, i + ua))
    send_b = pl.pallas_call(
        pack_rest,
        out_shape=sds((rows, 3 * UNIT * ub)),
        grid=(ub,),
        in_specs=[full((rows, rows)), part_b, part_b, part_b],
        out_specs=pl.BlockSpec((rows, 3 * UNIT), lambda i: (0, i)),
        compiler_params=params(),
        cost_estimate=cost(2 * rows * rows * 3 * UNIT * ub, 4 * rows * 3 * UNIT * ub),
        name="pack_rest",
    )(pick, q, k, v)
    recv_b = exchange(send_b)
    back = jnp.transpose(pick)

    def attention(recv, first, unit0, n_units):
        def col(m):
            return pl.BlockSpec((rows, UNIT), lambda i: (0, first + 3 * i + m))

        return pl.pallas_call(
            lambda *refs: attend(scale, *refs),
            out_shape=(sds((rows, 3 * UNIT * n_units)), sds((rows, UNIT * n_units))),
            grid=(n_units,),
            in_specs=[
                full((rows, width)),
                pl.BlockSpec((rows, LANES), lambda i: (0, wide_a // LANES - 1)),
                pl.BlockSpec((width, UNIT), lambda i: (0, i + unit0)),
                col(0),
                col(1),
                col(2),
            ],
            out_specs=(
                pl.BlockSpec((rows, 3 * UNIT), lambda i: (0, i)),
                pl.BlockSpec((rows, UNIT), lambda i: (0, i)),
            ),
            scratch_shapes=[pltpu.VMEM((rows, rows), F32)],
            compiler_params=params(),
            cost_estimate=cost(
                2 * rows * UNIT * n_units * (6 * rows + width),
                2 * rows * UNIT * n_units * 7 + 4 * rows * width,
                rows * rows * n_units * UNIT // HEAD_DIM,
            ),
            name="attend",
        )(recv_a, recv_a, w_out, recv, recv, recv)

    ret_a, att_a = attention(recv_a, width // UNIT, 0, ua)
    home_a = exchange(ret_a)
    ret_b, att_b = attention(recv_b, 0, ua, ub)
    home_b = exchange(ret_b)

    out_sds = (sds((rows, width)),) * 3
    outs = pl.pallas_call(
        lambda *refs: unpack(0, *refs),
        out_shape=out_sds,
        grid=(ua,),
        in_specs=[full((rows, rows)), pl.BlockSpec((rows, 3 * UNIT), lambda i: (0, i))],
        out_specs=(pl.BlockSpec((rows, UNIT), lambda i: (0, i)),) * 3,
        compiler_params=params(),
        cost_estimate=cost(2 * rows * rows * 3 * UNIT * ua, 4 * rows * 3 * UNIT * ua),
        name="unpack_a",
    )(back, home_a)
    outs = pl.pallas_call(
        lambda *refs: unpack(3, *refs),
        out_shape=out_sds,
        grid=(ub,),
        in_specs=[full((rows, rows)), pl.BlockSpec((rows, 3 * UNIT), lambda i: (0, i))]
        + [pl.BlockSpec(memory_space=pl.ANY)] * 3,
        out_specs=(pl.BlockSpec((rows, UNIT), lambda i: (0, i + ua)),) * 3,
        input_output_aliases={2: 0, 3: 1, 4: 2},
        compiler_params=params(),
        cost_estimate=cost(2 * rows * rows * 3 * UNIT * ub, 4 * rows * 3 * UNIT * ub),
        name="unpack_b",
    )(back, home_b, *outs)

    node = lax.axis_index("nodes")
    ix = lax.axis_index("rep")
    iy, iz, ic = node // (nz * nc), (node // nc) % nz, node % nc

    def nid(y, z, c):
        return ((y % ny) * nz + z % nz) * nc + c % nc

    everyone = [(y, z, c) for y in range(ny) for z in range(nz) for c in range(nc)]

    def hop(dy, dz, dc):
        return [(nid(y, z, c), nid(y + dy, z + dz, c + dc)) for y, z, c in everyone]

    def pick_of(array, index, axis):
        return lax.dynamic_index_in_dim(array, index, axis, keepdims=False)

    share = width // nx

    def reduced_over_chip_and_x(att):
        part = att.shape[1] // nx
        weight = tn(recv_a[:, :width], att)
        weight = weight.reshape(ny * nz, nc, width // node_count, att.shape[1])
        total = pick_of(weight, ic, 1)
        for s in range(1, nc):
            sent = pick_of(weight, (ic + s) % nc, 1).astype(BF)
            total = total + lax.ppermute(sent, "nodes", hop(0, 0, s))
        weight = total.reshape(width // nc, att.shape[1])
        came = []
        for s in range(1, nx):
            sent = lax.dynamic_slice_in_dim(weight, ((ix + s) % nx) * part, part, 1).astype(BF)
            came.append(lax.ppermute(sent, "rep", ring(nx, s)))
        total = lax.dynamic_slice_in_dim(weight, ix * part, part, 1)
        for piece in came:
            total = total + piece
        return lax.optimization_barrier(total)

    total_a = reduced_over_chip_and_x(att_a)
    att_b, total_a = lax.optimization_barrier((att_b, total_a))
    weight = jnp.concatenate([total_a, reduced_over_chip_and_x(att_b)], axis=1)
    weight = weight.reshape(ny, width // nc // ny, share)
    came = []
    for s in range(1, ny):
        sent = pick_of(weight, (iy + s) % ny, 0).astype(BF)
        came.append(lax.ppermute(sent, "nodes", hop(s, 0, 0)))
    total = pick_of(weight, iy, 0)
    for piece in came:
        total = total + piece
    low = lax.optimization_barrier(total).astype(BF)
    pieces = [low] + [lax.ppermute(low, "rep", ring(nx, nx - s)) for s in range(1, nx)]
    weight = lax.optimization_barrier(jnp.concatenate(pieces, axis=1))
    weight = weight.reshape(nz, width // node_count, width)
    shares = [pick_of(weight, iz, 0)]
    for s in range(1, nz):
        sent = pick_of(weight, (iz + s) % nz, 0)
        shares.append(lax.ppermute(sent, "nodes", hop(0, s, 0)))
    grad_weight = pl.pallas_call(
        lambda *refs: finish(norm_factor, nx, *refs),
        out_shape=sds((width // node_count, width), F32),
        in_specs=[pl.BlockSpec(memory_space=pltpu.SMEM)]
        + [pl.BlockSpec(memory_space=pltpu.VMEM)] * nz,
        cost_estimate=cost(0, 6 * width // node_count * width),
        name="finish",
    )(ix.reshape(1), *shares)
    return (outs[0][None], outs[1][None], outs[2][None], grad_weight)


def solution(mesh):
    nodes, nx = mesh.shape["nodes"], mesh.shape["rep"]
    nc = 2
    nz = 8
    ny = nodes // (nz * nc)
    in_specs = (
        P("rep", "nodes", None),
        P("rep", "nodes", None),
        P("rep", "nodes", None),
        P("rep", "nodes", None),
        P(),
        P("rep", "nodes"),
    )
    out_specs = (
        P("rep", "nodes", None),
        P("rep", "nodes", None),
        P("rep", "nodes", None),
        P("nodes", None),
    )

    def body(*args):
        return local((ny, nz, nc, nx), *args)

    return jax.shard_map(
        body, mesh=mesh, in_specs=in_specs, out_specs=out_specs, check_vma=False
    )
```

```python
import math

import jax
import jax.numpy as jnp
from jax import lax
from jax.experimental import pallas as pl
from jax.experimental.pallas import tpu as pltpu
from jax.sharding import PartitionSpec as P


HEAD_DIM = 128
CL_DEV = 4
UNIT = 256
UNITS_A = 2
LANES = 128
TAG_ROWS = 16
big_negative = -1e30
BF = jnp.bfloat16
F32 = jnp.float32


def mm(a, b, dims):
    return lax.dot_general(a, b, (dims, ((), ())), preferred_element_type=F32)


def nn(a, b):
    return mm(a, b, ((1,), (0,)))


def nt(a, b):
    return mm(a, b, ((1,), (1,)))


def tn(a, b):
    return mm(a, b, ((0,), (0,)))


def column_of(row, rows):
    return jnp.transpose(jnp.broadcast_to(row, (LANES, rows)))[:, :1]


def pack_first(rows, bucket, ids_ref, g_ref, q_ref, k_ref, v_ref, out_ref, pick_ref, tag_ref):
    ids_row = ids_ref[...].astype(F32)
    owner_row = jnp.floor(ids_row * (1.0 / CL_DEV))
    ids_col = column_of(ids_row, rows)
    owner_col = jnp.floor(ids_col * (1.0 / CL_DEV))
    tag_row = ids_row - owner_row * CL_DEV + 1.0
    down = lax.broadcasted_iota(jnp.int32, (rows, LANES), 0)
    across = lax.broadcasted_iota(jnp.int32, (rows, LANES), 1)

    @pl.loop(0, rows // LANES)
    def _(j):
        cols = pl.ds(pl.multiple_of(j * LANES, LANES), LANES)
        owner = jnp.floor(ids_ref[:, cols].astype(F32) * (1.0 / CL_DEV))
        same = (owner_col == owner) & (down < across + j * LANES)
        rank = jnp.sum(jnp.where(same, 1.0, 0.0), axis=0, keepdims=True)
        slot = (owner * bucket + rank).astype(jnp.int32)
        pick_ref[:, cols] = jnp.where(down == slot, 1.0, 0.0).astype(BF)

    width = g_ref.shape[1]

    def unit(n):
        return pl.ds(pl.multiple_of(n * UNIT, UNIT), UNIT)

    @pl.loop(0, width // UNIT)
    def _(u):
        out_ref[:, unit(u)] = nn(pick_ref[...], g_ref[:, unit(u)]).astype(BF)

    @pl.loop(0, q_ref.shape[1] // UNIT)
    def _(u):
        for m, ref in enumerate((q_ref, k_ref, v_ref)):
            base = width // UNIT + 3 * u + m
            out_ref[:, unit(base)] = nn(pick_ref[...], ref[:, unit(u)]).astype(BF)

    tags = jnp.broadcast_to(tag_row, (TAG_ROWS, rows)).astype(BF)
    tag_ref[...] = nt(tags, pick_ref[...])[:1].astype(BF)


def tag_order(sizes, bucket, at_ref, *refs):
    ny, nz, nc = sizes
    nodes = ny * nz * nc
    ins, out_ref = refs[:-1], refs[-1]
    iy, iz, ic = at_ref[0], at_ref[1], at_ref[2]
    table = jnp.concatenate([ref[...].astype(F32) for ref in ins], axis=0)
    rows = table.shape[1]
    lane = lax.broadcasted_iota(jnp.int32, (rows, LANES), 0)
    k = lax.broadcasted_iota(jnp.int32, (rows, LANES), 1)
    me = (iy * nz + iz) * nc + ic
    mine = jnp.where((lane == me * bucket + k) & (k < bucket), 1.0, 0.0).astype(BF)
    table = nn(table.astype(BF), mine)
    n = lax.broadcasted_iota(jnp.int32, (nodes, nodes), 0)
    at = lax.broadcasted_iota(jnp.int32, (nodes, nodes), 1)
    bits_c, bits_z = nc.bit_length() - 1, nz.bit_length() - 1
    dc = (ic - n) & (nc - 1)
    dz = (iz - (n >> bits_c)) & (nz - 1)
    dy = (iy - (n >> (bits_c + bits_z))) & (ny - 1)
    turn = jnp.where(at == (dz * ny + dy) * nc + dc, 1.0, 0.0).astype(BF)
    table = nn(turn, table.astype(BF)).astype(BF)
    n = lax.broadcasted_iota(jnp.int32, (nodes, rows), 0)
    slot = lax.broadcasted_iota(jnp.int32, (nodes, rows), 1)
    bits_k = bucket.bit_length() - 1
    spread = tn(table, jnp.where((slot >> bits_k) == n, 1.0, 0.0).astype(BF))
    k = lax.broadcasted_iota(jnp.int32, spread.shape, 0)
    slot = lax.broadcasted_iota(jnp.int32, spread.shape, 1)
    kept = jnp.where((slot & (bucket - 1)) == k, spread, 0.0)
    out_ref[...] = jnp.sum(kept, axis=0, keepdims=True)


def pack_rest(pick_ref, q_ref, k_ref, v_ref, out_ref):
    pick = pick_ref[...]
    for m, ref in enumerate((q_ref, k_ref, v_ref)):
        out_ref[:, m * UNIT : (m + 1) * UNIT] = nn(pick, ref[...]).astype(BF)


def attend(scale, g_ref, tag_ref, w_ref, q_ref, k_ref, v_ref, ret_ref, att_ref, bias_ref):
    rows = g_ref.shape[0]

    @pl.when(pl.program_id(0) == 0)
    def _():
        tags = column_of(tag_ref[...], rows)

        @pl.loop(0, rows // LANES)
        def _(j):
            cols = pl.ds(pl.multiple_of(j * LANES, LANES), LANES)
            bias_ref[:, cols] = jnp.where(tags == tag_ref[:, cols], 0.0, big_negative)

    q, k, v = q_ref[...], k_ref[...], v_ref[...]
    grad = nn(g_ref[...], w_ref[...]).astype(BF)
    scores = nt(q, k) * scale + bias_ref[...]
    weights = jnp.exp(scores - jnp.max(scores, axis=1, keepdims=True))
    probs = weights * (1.0 / jnp.sum(weights, axis=1, keepdims=True))
    low = probs.astype(BF)
    attended = nn(low, v).astype(BF)
    delta = jnp.sum(grad.astype(F32) * attended.astype(F32), axis=1, keepdims=True)
    grad_scores = (probs * (nt(grad, v) - delta) * scale).astype(BF)
    att_ref[...] = attended
    for m, part in enumerate((nn(grad_scores, k), tn(grad_scores, q), tn(low, grad))):
        ret_ref[:, m * HEAD_DIM : (m + 1) * HEAD_DIM] = part.astype(BF)


def unpack(held, back_ref, ret_ref, *refs):
    outs = refs[held:]
    rows_out = nn(back_ref[...], ret_ref[...]).astype(BF)
    for h in range(UNIT // HEAD_DIM):
        for m, ref in enumerate(outs):
            cols = slice(h * HEAD_DIM, (h + 1) * HEAD_DIM)
            base = (h * len(outs) + m) * HEAD_DIM
            ref[:, cols] = rows_out[:, base : base + HEAD_DIM]


def finish(factor, nx, at_ref, *refs):
    ins, out_ref = refs[:-1], refs[-1]
    total = ins[0][...].astype(F32)
    for ref in ins[1:]:
        total = total + ref[...].astype(F32)
    total = total * factor
    half = total.shape[1] // nx // 2
    for s in range(nx):
        source = lax.rem(at_ref[0] + s, nx)
        for m in range(2):
            cols = pl.ds(pl.multiple_of((m * nx + source) * half, half), half)
            base = (2 * s + m) * half
            out_ref[:, cols] = total[:, base : base + half]


def cost(flops, nbytes, exps=0):
    return pl.CostEstimate(flops=flops, bytes_accessed=nbytes, transcendentals=exps)


def params():
    return pltpu.CompilerParams(vmem_limit_bytes=67043328)


def ring(size, shift):
    return [(i, (i + shift) % size) for i in range(size)]


def local(sizes, queries, keys, values, grad_out, w_out, cluster_id):
    ny, nz, nc, nx = sizes
    node_count = ny * nz * nc
    rows = queries.shape[1]
    width = queries.shape[2]
    bucket = rows // node_count
    units = width // UNIT
    ua, ub = UNITS_A, units - UNITS_A
    scale = 1.0 / math.sqrt(HEAD_DIM)
    norm_factor = 1.0 / math.sqrt(nx * node_count * rows)
    q, k, v, g = queries[0], keys[0], values[0], grad_out[0]

    def sds(shape, dtype=BF):
        return jax.ShapeDtypeStruct(shape, dtype)

    def full(shape):
        return pl.BlockSpec(shape, lambda *_: (0,) * len(shape))

    def exchange(rows_in):
        c = rows_in.shape[1]
        out = lax.all_to_all(
            rows_in.reshape(node_count, bucket, c),
            "nodes",
            split_axis=0,
            concat_axis=0,
            tiled=True,
        )
        return out.reshape(rows, c)

    wide_a = width + 3 * UNIT * ua
    part_a = pl.BlockSpec((rows, UNIT * ua), lambda i: (0, 0))
    send_a, pick, tags = pl.pallas_call(
        lambda *refs: pack_first(rows, bucket, *refs),
        out_shape=(sds((rows, wide_a)), sds((rows, rows)), sds((1, rows))),
        grid=(1,),
        in_specs=[full((1, rows)), full((rows, width)), part_a, part_a, part_a],
        out_specs=(full((rows, wide_a)), full((rows, rows)), full((1, rows))),
        compiler_params=params(),
        cost_estimate=cost(2 * rows * rows * wide_a, 4 * rows * wide_a),
        name="pack_first",
    )(cluster_id, g, q, k, v)
    recv_a = exchange(send_a)

    node = lax.axis_index("nodes")
    ix = lax.axis_index("rep")
    iy, iz, ic = node // (nz * nc), (node // nc) % nz, node % nc

    def nid(y, z, c):
        return ((y % ny) * nz + z % nz) * nc + c % nc

    everyone = [(y, z, c) for y in range(ny) for z in range(nz) for c in range(nc)]

    def hop(dy, dz, dc):
        return [(nid(y, z, c), nid(y + dy, z + dz, c + dc)) for y, z, c in everyone]

    def pick_of(array, index, axis):
        return lax.dynamic_index_in_dim(array, index, axis, keepdims=False)

    def around(line, count, step):
        return [line] + [lax.ppermute(line, "nodes", hop(*step(s))) for s in range(1, count)]

    line = jnp.concatenate(around(tags, nc, lambda s: (0, 0, s)), axis=0)
    step = 1
    while step < ny:
        line = jnp.concatenate([line, lax.ppermute(line, "nodes", hop(step, 0, 0))], axis=0)
        step *= 2
    lines = around(line, nz, lambda s: (0, s, 0))
    tag_line = pl.pallas_call(
        lambda *refs: tag_order((ny, nz, nc), bucket, *refs),
        out_shape=sds((1, rows), F32),
        in_specs=[pl.BlockSpec(memory_space=pltpu.SMEM)]
        + [pl.BlockSpec(memory_space=pltpu.VMEM)] * nz,
        cost_estimate=cost(2 * rows * rows * LANES, 4 * rows * rows),
        name="tag_order",
    )(jnp.stack([iy, iz, ic]), *lines)

    part_b = pl.BlockSpec((rows, UNIT), lambda i: (0, i + ua))
    send_b = pl.pallas_call(
        pack_rest,
        out_shape=sds((rows, 3 * UNIT * ub)),
        grid=(ub,),
        in_specs=[full((rows, rows)), part_b, part_b, part_b],
        out_specs=pl.BlockSpec((rows, 3 * UNIT), lambda i: (0, i)),
        compiler_params=params(),
        cost_estimate=cost(2 * rows * rows * 3 * UNIT * ub, 4 * rows * 3 * UNIT * ub),
        name="pack_rest",
    )(pick, q, k, v)
    recv_b = exchange(send_b)
    back = jnp.transpose(pick)

    def attention(recv, first, unit0, n_units):
        per = UNIT // HEAD_DIM

        def col(m):
            return pl.BlockSpec(
                (rows, HEAD_DIM), lambda i: (0, per * (first + 3 * (i // per) + m) + i % per)
            )

        return pl.pallas_call(
            lambda *refs: attend(scale, *refs),
            out_shape=(sds((rows, 3 * UNIT * n_units)), sds((rows, UNIT * n_units))),
            grid=(n_units * per,),
            in_specs=[
                full((rows, width)),
                full((1, rows)),
                pl.BlockSpec((width, HEAD_DIM), lambda i: (0, i + unit0 * per)),
                col(0),
                col(1),
                col(2),
            ],
            out_specs=(
                pl.BlockSpec((rows, 3 * HEAD_DIM), lambda i: (0, i)),
                pl.BlockSpec((rows, HEAD_DIM), lambda i: (0, i)),
            ),
            scratch_shapes=[pltpu.VMEM((rows, rows), F32)],
            compiler_params=params(),
            cost_estimate=cost(
                2 * rows * UNIT * n_units * (6 * rows + width),
                2 * rows * UNIT * n_units * 7 + 4 * rows * width,
                rows * rows * n_units * UNIT // HEAD_DIM,
            ),
            name="attend",
        )(recv_a, tag_line, w_out, recv, recv, recv)

    ret_a, att_a = attention(recv_a, width // UNIT, 0, ua)
    home_a = exchange(ret_a)
    ret_b, att_b = attention(recv_b, 0, ua, ub)
    home_b = exchange(ret_b)

    out_sds = (sds((rows, width)),) * 3
    outs = pl.pallas_call(
        lambda *refs: unpack(0, *refs),
        out_shape=out_sds,
        grid=(ua,),
        in_specs=[full((rows, rows)), pl.BlockSpec((rows, 3 * UNIT), lambda i: (0, i))],
        out_specs=(pl.BlockSpec((rows, UNIT), lambda i: (0, i)),) * 3,
        compiler_params=params(),
        cost_estimate=cost(2 * rows * rows * 3 * UNIT * ua, 4 * rows * 3 * UNIT * ua),
        name="unpack_a",
    )(back, home_a)
    outs = pl.pallas_call(
        lambda *refs: unpack(3, *refs),
        out_shape=out_sds,
        grid=(ub,),
        in_specs=[full((rows, rows)), pl.BlockSpec((rows, 3 * UNIT), lambda i: (0, i))]
        + [pl.BlockSpec(memory_space=pl.ANY)] * 3,
        out_specs=(pl.BlockSpec((rows, UNIT), lambda i: (0, i + ua)),) * 3,
        input_output_aliases={2: 0, 3: 1, 4: 2},
        compiler_params=params(),
        cost_estimate=cost(2 * rows * rows * 3 * UNIT * ub, 4 * rows * 3 * UNIT * ub),
        name="unpack_b",
    )(back, home_b, *outs)

    share = width // nx

    def reduced_over_chip_and_x(att):
        part = att.shape[1] // nx
        weight = tn(recv_a[:, :width], att)
        weight = weight.reshape(ny * nz, nc, width // node_count, att.shape[1])
        total = pick_of(weight, ic, 1)
        for s in range(1, nc):
            sent = pick_of(weight, (ic + s) % nc, 1).astype(BF)
            total = total + lax.ppermute(sent, "nodes", hop(0, 0, s))
        weight = total.reshape(width // nc, att.shape[1])
        came = []
        for s in range(1, nx):
            sent = lax.dynamic_slice_in_dim(weight, ((ix + s) % nx) * part, part, 1).astype(BF)
            came.append(lax.ppermute(sent, "rep", ring(nx, s)))
        total = lax.dynamic_slice_in_dim(weight, ix * part, part, 1)
        for piece in came:
            total = total + piece
        return lax.optimization_barrier(total)

    total_a = reduced_over_chip_and_x(att_a)
    att_b, total_a = lax.optimization_barrier((att_b, total_a))
    weight = jnp.concatenate([total_a, reduced_over_chip_and_x(att_b)], axis=1)
    weight = weight.reshape(ny, width // nc // ny, share)
    came = []
    for s in range(1, ny):
        sent = pick_of(weight, (iy + s) % ny, 0).astype(BF)
        came.append(lax.ppermute(sent, "nodes", hop(s, 0, 0)))
    total = pick_of(weight, iy, 0)
    for piece in came:
        total = total + piece
    low = lax.optimization_barrier(total).astype(BF)
    pieces = [low] + [lax.ppermute(low, "rep", ring(nx, nx - s)) for s in range(1, nx)]
    weight = lax.optimization_barrier(jnp.concatenate(pieces, axis=1))
    weight = weight.reshape(nz, width // node_count, width)
    shares = [pick_of(weight, iz, 0)]
    for s in range(1, nz):
        sent = pick_of(weight, (iz + s) % nz, 0)
        shares.append(lax.ppermute(sent, "nodes", hop(0, s, 0)))
    grad_weight = pl.pallas_call(
        lambda *refs: finish(norm_factor, nx, *refs),
        out_shape=sds((width // node_count, width), F32),
        in_specs=[pl.BlockSpec(memory_space=pltpu.SMEM)]
        + [pl.BlockSpec(memory_space=pltpu.VMEM)] * nz,
        cost_estimate=cost(0, 6 * width // node_count * width),
        name="finish",
    )(ix.reshape(1), *shares)
    return (outs[0][None], outs[1][None], outs[2][None], grad_weight)


def solution(mesh):
    nodes, nx = mesh.shape["nodes"], mesh.shape["rep"]
    nc = 2
    nz = 8
    ny = nodes // (nz * nc)
    in_specs = (
        P("rep", "nodes", None),
        P("rep", "nodes", None),
        P("rep", "nodes", None),
        P("rep", "nodes", None),
        P(),
        P("rep", "nodes"),
    )
    out_specs = (
        P("rep", "nodes", None),
        P("rep", "nodes", None),
        P("rep", "nodes", None),
        P("nodes", None),
    )

    def body(*args):
        return local((ny, nz, nc, nx), *args)

    return jax.shard_map(
        body, mesh=mesh, in_specs=in_specs, out_specs=out_specs, check_vma=False
    )
```

```python
import math

import jax
import jax.numpy as jnp
from jax import lax
from jax.experimental import pallas as pl
from jax.experimental.pallas import tpu as pltpu
from jax.sharding import PartitionSpec as P


HEAD_DIM = 128
CL_DEV = 4
UNIT = 256
UNITS_A = 2
LANES = 128
TAG_ROWS = 16
big_negative = -1e30
BF = jnp.bfloat16
F32 = jnp.float32


def mm(a, b, dims):
    return lax.dot_general(a, b, (dims, ((), ())), preferred_element_type=F32)


def nn(a, b):
    return mm(a, b, ((1,), (0,)))


def nt(a, b):
    return mm(a, b, ((1,), (1,)))


def tn(a, b):
    return mm(a, b, ((0,), (0,)))


def column_of(row, rows):
    return jnp.transpose(jnp.broadcast_to(row, (LANES, rows)))[:, :1]


def pack_first(rows, bucket, ids_ref, g_ref, q_ref, k_ref, v_ref, out_ref, pick_ref, tag_ref):
    ids_row = ids_ref[...].astype(F32)
    owner_row = jnp.floor(ids_row * (1.0 / CL_DEV))
    ids_col = column_of(ids_row, rows)
    owner_col = jnp.floor(ids_col * (1.0 / CL_DEV))
    tag_row = ids_row - owner_row * CL_DEV + 1.0
    down = lax.broadcasted_iota(jnp.int32, (rows, rows), 0)
    across = lax.broadcasted_iota(jnp.int32, (rows, rows), 1)
    same = (owner_col == owner_row) & (down < across)
    rank = jnp.sum(jnp.where(same, 1.0, 0.0), axis=0, keepdims=True)
    slot = (owner_row * bucket + rank).astype(jnp.int32)
    pick = jnp.where(down == slot, 1.0, 0.0).astype(BF)
    pick_ref[...] = pick
    tags = jnp.broadcast_to(tag_row, (TAG_ROWS, rows)).astype(BF)
    tag_ref[...] = nt(tags, pick)[:1].astype(BF)
    width = g_ref.shape[1]
    out_ref[:, :width] = nn(pick, g_ref[...]).astype(BF)
    for u in range(q_ref.shape[1] // UNIT):
        for m, ref in enumerate((q_ref, k_ref, v_ref)):
            base = width + (3 * u + m) * UNIT
            out_ref[:, base : base + UNIT] = nn(pick, ref[:, u * UNIT : (u + 1) * UNIT]).astype(BF)


def tag_order(sizes, bucket, at_ref, *refs):
    ny, nz, nc = sizes
    nodes = ny * nz * nc
    ins, out_ref = refs[:-1], refs[-1]
    iy, iz, ic = at_ref[0], at_ref[1], at_ref[2]
    table = jnp.concatenate([ref[...].astype(F32) for ref in ins], axis=0)
    rows = table.shape[1]
    lane = lax.broadcasted_iota(jnp.int32, (rows, LANES), 0)
    k = lax.broadcasted_iota(jnp.int32, (rows, LANES), 1)
    me = (iy * nz + iz) * nc + ic
    mine = jnp.where((lane == me * bucket + k) & (k < bucket), 1.0, 0.0).astype(BF)
    table = nn(table.astype(BF), mine)
    n = lax.broadcasted_iota(jnp.int32, (nodes, nodes), 0)
    at = lax.broadcasted_iota(jnp.int32, (nodes, nodes), 1)
    bits_c, bits_z = nc.bit_length() - 1, nz.bit_length() - 1
    dc = (ic - n) & (nc - 1)
    dz = (iz - (n >> bits_c)) & (nz - 1)
    dy = (iy - (n >> (bits_c + bits_z))) & (ny - 1)
    turn = jnp.where(at == (dz * ny + dy) * nc + dc, 1.0, 0.0).astype(BF)
    table = nn(turn, table.astype(BF)).astype(BF)
    n = lax.broadcasted_iota(jnp.int32, (nodes, rows), 0)
    slot = lax.broadcasted_iota(jnp.int32, (nodes, rows), 1)
    bits_k = bucket.bit_length() - 1
    spread = tn(table, jnp.where((slot >> bits_k) == n, 1.0, 0.0).astype(BF))
    k = lax.broadcasted_iota(jnp.int32, spread.shape, 0)
    slot = lax.broadcasted_iota(jnp.int32, spread.shape, 1)
    kept = jnp.where((slot & (bucket - 1)) == k, spread, 0.0)
    out_ref[...] = jnp.sum(kept, axis=0, keepdims=True)


def pack_rest(pick_ref, q_ref, k_ref, v_ref, out_ref):
    pick = pick_ref[...]
    for m, ref in enumerate((q_ref, k_ref, v_ref)):
        out_ref[:, m * UNIT : (m + 1) * UNIT] = nn(pick, ref[...]).astype(BF)


def attend(scale, g_ref, tag_ref, w_ref, q_ref, k_ref, v_ref, ret_ref, att_ref, bias_ref):
    rows = g_ref.shape[0]

    @pl.when(pl.program_id(0) == 0)
    def _():
        tags = column_of(tag_ref[...], rows)

        @pl.loop(0, rows // LANES)
        def _(j):
            cols = pl.ds(pl.multiple_of(j * LANES, LANES), LANES)
            bias_ref[:, cols] = jnp.where(tags == tag_ref[:, cols], 0.0, big_negative)

    q, k, v = q_ref[...], k_ref[...], v_ref[...]
    grad = nn(g_ref[...], w_ref[...]).astype(BF)
    scores = nt(q, k) * scale + bias_ref[...]
    weights = jnp.exp(scores - jnp.max(scores, axis=1, keepdims=True))
    probs = weights * (1.0 / jnp.sum(weights, axis=1, keepdims=True))
    low = probs.astype(BF)
    attended = nn(low, v).astype(BF)
    delta = jnp.sum(grad.astype(F32) * attended.astype(F32), axis=1, keepdims=True)
    grad_scores = (probs * (nt(grad, v) - delta) * scale).astype(BF)
    att_ref[...] = attended
    for m, part in enumerate((nn(grad_scores, k), tn(grad_scores, q), tn(low, grad))):
        ret_ref[:, m * HEAD_DIM : (m + 1) * HEAD_DIM] = part.astype(BF)


def unpack(held, back_ref, ret_ref, *refs):
    outs = refs[held:]
    rows_out = nn(back_ref[...], ret_ref[...]).astype(BF)
    for h in range(UNIT // HEAD_DIM):
        for m, ref in enumerate(outs):
            cols = slice(h * HEAD_DIM, (h + 1) * HEAD_DIM)
            base = (h * len(outs) + m) * HEAD_DIM
            ref[:, cols] = rows_out[:, base : base + HEAD_DIM]


def finish(factor, nx, at_ref, *refs):
    ins, out_ref = refs[:-1], refs[-1]
    total = ins[0][...].astype(F32)
    for ref in ins[1:]:
        total = total + ref[...].astype(F32)
    total = total * factor
    half = total.shape[1] // nx // 2
    for s in range(nx):
        source = at_ref[0] ^ (s ^ (s >> 1))
        for m in range(2):
            cols = pl.ds(pl.multiple_of((m * nx + source) * half, half), half)
            base = (2 * s + m) * half
            out_ref[:, cols] = total[:, base : base + half]


def cost(flops, nbytes, exps=0):
    return pl.CostEstimate(flops=flops, bytes_accessed=nbytes, transcendentals=exps)


def params():
    return pltpu.CompilerParams(vmem_limit_bytes=67043328)


def ring(size, shift):
    return [(i, (i + shift) % size) for i in range(size)]


def local(sizes, queries, keys, values, grad_out, w_out, cluster_id):
    ny, nz, nc, nx = sizes
    node_count = ny * nz * nc
    rows = queries.shape[1]
    width = queries.shape[2]
    bucket = rows // node_count
    units = width // UNIT
    ua, ub = UNITS_A, units - UNITS_A
    scale = 1.0 / math.sqrt(HEAD_DIM)
    norm_factor = 1.0 / math.sqrt(nx * node_count * rows)
    q, k, v, g = queries[0], keys[0], values[0], grad_out[0]

    def sds(shape, dtype=BF):
        return jax.ShapeDtypeStruct(shape, dtype)

    def full(shape):
        return pl.BlockSpec(shape, lambda *_: (0,) * len(shape))

    def exchange(rows_in):
        c = rows_in.shape[1]
        out = lax.all_to_all(
            rows_in.reshape(node_count, bucket, c),
            "nodes",
            split_axis=0,
            concat_axis=0,
            tiled=True,
        )
        return out.reshape(rows, c)

    wide_a = width + 3 * UNIT * ua
    part_a = pl.BlockSpec((rows, UNIT * ua), lambda i: (0, 0))
    send_a, pick, tags = pl.pallas_call(
        lambda *refs: pack_first(rows, bucket, *refs),
        out_shape=(sds((rows, wide_a)), sds((rows, rows)), sds((1, rows))),
        grid=(1,),
        in_specs=[full((1, rows)), full((rows, width)), part_a, part_a, part_a],
        out_specs=(full((rows, wide_a)), full((rows, rows)), full((1, rows))),
        compiler_params=params(),
        cost_estimate=cost(2 * rows * rows * wide_a, 4 * rows * wide_a),
        name="pack_first",
    )(cluster_id, g, q, k, v)
    recv_a = exchange(send_a)

    node = lax.axis_index("nodes")
    ix = lax.axis_index("rep")
    iy, iz, ic = node // (nz * nc), (node // nc) % nz, node % nc

    def nid(y, z, c):
        return ((y % ny) * nz + z % nz) * nc + c % nc

    everyone = [(y, z, c) for y in range(ny) for z in range(nz) for c in range(nc)]

    def hop(dy, dz, dc):
        return [(nid(y, z, c), nid(y + dy, z + dz, c + dc)) for y, z, c in everyone]

    def pick_of(array, index, axis):
        return lax.dynamic_index_in_dim(array, index, axis, keepdims=False)

    def around(line, count, step):
        return [line] + [lax.ppermute(line, "nodes", hop(*step(s))) for s in range(1, count)]

    line = jnp.concatenate(around(tags, nc, lambda s: (0, 0, s)), axis=0)
    step = 1
    while step < ny:
        line = jnp.concatenate([line, lax.ppermute(line, "nodes", hop(step, 0, 0))], axis=0)
        step *= 2
    lines = around(line, nz, lambda s: (0, s, 0))
    tag_line = pl.pallas_call(
        lambda *refs: tag_order((ny, nz, nc), bucket, *refs),
        out_shape=sds((1, rows), F32),
        in_specs=[pl.BlockSpec(memory_space=pltpu.SMEM)]
        + [pl.BlockSpec(memory_space=pltpu.VMEM)] * nz,
        cost_estimate=cost(2 * rows * rows * LANES, 4 * rows * rows),
        name="tag_order",
    )(jnp.stack([iy, iz, ic]), *lines)

    part_b = pl.BlockSpec((rows, UNIT), lambda i: (0, i + ua))
    send_b = pl.pallas_call(
        pack_rest,
        out_shape=sds((rows, 3 * UNIT * ub)),
        grid=(ub,),
        in_specs=[full((rows, rows)), part_b, part_b, part_b],
        out_specs=pl.BlockSpec((rows, 3 * UNIT), lambda i: (0, i)),
        compiler_params=params(),
        cost_estimate=cost(2 * rows * rows * 3 * UNIT * ub, 4 * rows * 3 * UNIT * ub),
        name="pack_rest",
    )(pick, q, k, v)
    recv_b = exchange(send_b)
    back = jnp.transpose(pick)

    def attention(recv, first, unit0, n_units):
        per = UNIT // HEAD_DIM

        def col(m):
            return pl.BlockSpec(
                (rows, HEAD_DIM), lambda i: (0, per * (first + 3 * (i // per) + m) + i % per)
            )

        return pl.pallas_call(
            lambda *refs: attend(scale, *refs),
            out_shape=(sds((rows, 3 * UNIT * n_units)), sds((rows, UNIT * n_units))),
            grid=(n_units * per,),
            in_specs=[
                full((rows, width)),
                full((1, rows)),
                pl.BlockSpec((width, HEAD_DIM), lambda i: (0, i + unit0 * per)),
                col(0),
                col(1),
                col(2),
            ],
            out_specs=(
                pl.BlockSpec((rows, 3 * HEAD_DIM), lambda i: (0, i)),
                pl.BlockSpec((rows, HEAD_DIM), lambda i: (0, i)),
            ),
            scratch_shapes=[pltpu.VMEM((rows, rows), F32)],
            compiler_params=params(),
            cost_estimate=cost(
                2 * rows * UNIT * n_units * (6 * rows + width),
                2 * rows * UNIT * n_units * 7 + 4 * rows * width,
                rows * rows * n_units * UNIT // HEAD_DIM,
            ),
            name="attend",
        )(recv_a, tag_line, w_out, recv, recv, recv)

    ret_a, att_a = attention(recv_a, width // UNIT, 0, ua)
    home_a = exchange(ret_a)
    ret_b, att_b = attention(recv_b, 0, ua, ub)
    home_b = exchange(ret_b)

    out_sds = (sds((rows, width)),) * 3
    outs = pl.pallas_call(
        lambda *refs: unpack(0, *refs),
        out_shape=out_sds,
        grid=(ua,),
        in_specs=[full((rows, rows)), pl.BlockSpec((rows, 3 * UNIT), lambda i: (0, i))],
        out_specs=(pl.BlockSpec((rows, UNIT), lambda i: (0, i)),) * 3,
        compiler_params=params(),
        cost_estimate=cost(2 * rows * rows * 3 * UNIT * ua, 4 * rows * 3 * UNIT * ua),
        name="unpack_a",
    )(back, home_a)
    outs = pl.pallas_call(
        lambda *refs: unpack(3, *refs),
        out_shape=out_sds,
        grid=(ub,),
        in_specs=[full((rows, rows)), pl.BlockSpec((rows, 3 * UNIT), lambda i: (0, i))]
        + [pl.BlockSpec(memory_space=pl.ANY)] * 3,
        out_specs=(pl.BlockSpec((rows, UNIT), lambda i: (0, i + ua)),) * 3,
        input_output_aliases={2: 0, 3: 1, 4: 2},
        compiler_params=params(),
        cost_estimate=cost(2 * rows * rows * 3 * UNIT * ub, 4 * rows * 3 * UNIT * ub),
        name="unpack_b",
    )(back, home_b, *outs)

    share = width // nx

    def reduced_over_chip_and_x(att):
        part = att.shape[1] // nx
        weight = tn(recv_a[:, :width], att)
        weight = weight.reshape(ny * nz, nc, width // node_count, att.shape[1])
        total = pick_of(weight, ic, 1)
        for s in range(1, nc):
            sent = pick_of(weight, (ic + s) % nc, 1).astype(BF)
            total = total + lax.ppermute(sent, "nodes", hop(0, 0, s))
        weight = total.reshape(width // nc, att.shape[1])
        came = []
        for s in range(1, nx):
            sent = lax.dynamic_slice_in_dim(weight, ((ix + s) % nx) * part, part, 1).astype(BF)
            came.append(lax.ppermute(sent, "rep", ring(nx, s)))
        total = lax.dynamic_slice_in_dim(weight, ix * part, part, 1)
        for piece in came:
            total = total + piece
        return lax.optimization_barrier(total)

    total_a = reduced_over_chip_and_x(att_a)
    att_b, total_a = lax.optimization_barrier((att_b, total_a))
    weight = jnp.concatenate([total_a, reduced_over_chip_and_x(att_b)], axis=1)
    weight = weight.reshape(ny, width // nc // ny, share)
    came = []
    for s in range(1, ny):
        sent = pick_of(weight, (iy + s) % ny, 0).astype(BF)
        came.append(lax.ppermute(sent, "nodes", hop(s, 0, 0)))
    total = pick_of(weight, iy, 0)
    for piece in came:
        total = total + piece
    low = lax.optimization_barrier(total).astype(BF)
    held, turn = 1, low
    while held < nx:
        mask = 2 * held - 1
        came = lax.ppermute(turn, "rep", [(i, i ^ mask) for i in range(nx)])
        turn = jnp.concatenate([turn, came], axis=1)
        held *= 2
    weight = lax.optimization_barrier(turn)
    weight = weight.reshape(nz, width // node_count, width)
    shares = [pick_of(weight, iz, 0)]
    for s in range(1, nz):
        sent = pick_of(weight, (iz + s) % nz, 0)
        shares.append(lax.ppermute(sent, "nodes", hop(0, s, 0)))
    grad_weight = pl.pallas_call(
        lambda *refs: finish(norm_factor, nx, *refs),
        out_shape=sds((width // node_count, width), F32),
        in_specs=[pl.BlockSpec(memory_space=pltpu.SMEM)]
        + [pl.BlockSpec(memory_space=pltpu.VMEM)] * nz,
        cost_estimate=cost(0, 6 * width // node_count * width),
        name="finish",
    )(ix.reshape(1), *shares)
    return (outs[0][None], outs[1][None], outs[2][None], grad_weight)


def solution(mesh):
    nodes, nx = mesh.shape["nodes"], mesh.shape["rep"]
    nc = 2
    nz = 8
    ny = nodes // (nz * nc)
    in_specs = (
        P("rep", "nodes", None),
        P("rep", "nodes", None),
        P("rep", "nodes", None),
        P("rep", "nodes", None),
        P(),
        P("rep", "nodes"),
    )
    out_specs = (
        P("rep", "nodes", None),
        P("rep", "nodes", None),
        P("rep", "nodes", None),
        P("nodes", None),
    )

    def body(*args):
        return local((ny, nz, nc, nx), *args)

    return jax.shard_map(
        body, mesh=mesh, in_specs=in_specs, out_specs=out_specs, check_vma=False
    )
```

```python
import math

import jax
import jax.numpy as jnp
from jax import lax
from jax.experimental import pallas as pl
from jax.experimental.pallas import tpu as pltpu
from jax.sharding import PartitionSpec as P


HEAD_DIM = 128
CL_DEV = 4
UNIT = 256
UNITS_A = 3
LANES = 128
TAG_ROWS = 16
big_negative = -1e30
BF = jnp.bfloat16
F32 = jnp.float32


def mm(a, b, dims):
    return lax.dot_general(a, b, (dims, ((), ())), preferred_element_type=F32)


def nn(a, b):
    return mm(a, b, ((1,), (0,)))


def nt(a, b):
    return mm(a, b, ((1,), (1,)))


def tn(a, b):
    return mm(a, b, ((0,), (0,)))


def column_of(row, rows):
    return jnp.transpose(jnp.broadcast_to(row, (LANES, rows)))[:, :1]


def pack_first(rows, bucket, ids_ref, g_ref, q_ref, k_ref, v_ref, out_ref, pick_ref, tag_ref):
    ids_row = ids_ref[...].astype(F32)
    owner_row = jnp.floor(ids_row * (1.0 / CL_DEV))
    ids_col = column_of(ids_row, rows)
    owner_col = jnp.floor(ids_col * (1.0 / CL_DEV))
    tag_row = ids_row - owner_row * CL_DEV + 1.0
    down = lax.broadcasted_iota(jnp.int32, (rows, rows), 0)
    across = lax.broadcasted_iota(jnp.int32, (rows, rows), 1)
    same = (owner_col == owner_row) & (down < across)
    rank = jnp.sum(jnp.where(same, 1.0, 0.0), axis=0, keepdims=True)
    slot = (owner_row * bucket + rank).astype(jnp.int32)
    pick = jnp.where(down == slot, 1.0, 0.0).astype(BF)
    pick_ref[...] = pick
    tags = jnp.broadcast_to(tag_row, (TAG_ROWS, rows)).astype(BF)
    tag_ref[...] = nt(tags, pick)[:1].astype(BF)
    width = g_ref.shape[1]
    out_ref[:, :width] = nn(pick, g_ref[...]).astype(BF)
    for u in range(q_ref.shape[1] // UNIT):
        for m, ref in enumerate((q_ref, k_ref, v_ref)):
            base = width + (3 * u + m) * UNIT
            out_ref[:, base : base + UNIT] = nn(pick, ref[:, u * UNIT : (u + 1) * UNIT]).astype(BF)


def tag_order(sizes, bucket, at_ref, *refs):
    ny, nz, nc = sizes
    nodes = ny * nz * nc
    ins, out_ref = refs[:-1], refs[-1]
    iy, iz, ic = at_ref[0], at_ref[1], at_ref[2]
    table = jnp.concatenate([ref[...].astype(F32) for ref in ins], axis=0)
    rows = table.shape[1]
    lane = lax.broadcasted_iota(jnp.int32, (rows, LANES), 0)
    k = lax.broadcasted_iota(jnp.int32, (rows, LANES), 1)
    me = (iy * nz + iz) * nc + ic
    mine = jnp.where((lane == me * bucket + k) & (k < bucket), 1.0, 0.0).astype(BF)
    table = nn(table.astype(BF), mine)
    n = lax.broadcasted_iota(jnp.int32, (nodes, nodes), 0)
    at = lax.broadcasted_iota(jnp.int32, (nodes, nodes), 1)
    bits_c, bits_z = nc.bit_length() - 1, nz.bit_length() - 1
    dc = (ic - n) & (nc - 1)
    dz = (iz - (n >> bits_c)) & (nz - 1)
    dy = (iy - (n >> (bits_c + bits_z))) & (ny - 1)
    turn = jnp.where(at == (dz * ny + dy) * nc + dc, 1.0, 0.0).astype(BF)
    table = nn(turn, table.astype(BF)).astype(BF)
    n = lax.broadcasted_iota(jnp.int32, (nodes, rows), 0)
    slot = lax.broadcasted_iota(jnp.int32, (nodes, rows), 1)
    bits_k = bucket.bit_length() - 1
    spread = tn(table, jnp.where((slot >> bits_k) == n, 1.0, 0.0).astype(BF))
    k = lax.broadcasted_iota(jnp.int32, spread.shape, 0)
    slot = lax.broadcasted_iota(jnp.int32, spread.shape, 1)
    kept = jnp.where((slot & (bucket - 1)) == k, spread, 0.0)
    out_ref[...] = jnp.sum(kept, axis=0, keepdims=True)


def pack_rest(pick_ref, q_ref, k_ref, v_ref, out_ref):
    pick = pick_ref[...]
    for m, ref in enumerate((q_ref, k_ref, v_ref)):
        out_ref[:, m * UNIT : (m + 1) * UNIT] = nn(pick, ref[...]).astype(BF)


def attend(scale, g_ref, tag_ref, w_ref, q_ref, k_ref, v_ref, *refs):
    ret_ref, att_ref, bias_ref = refs[-3:]
    rows = g_ref.shape[0]

    @pl.when(pl.program_id(0) == 0)
    def _():
        tags = column_of(tag_ref[...], rows)

        @pl.loop(0, rows // LANES)
        def _(j):
            cols = pl.ds(pl.multiple_of(j * LANES, LANES), LANES)
            bias_ref[:, cols] = jnp.where(tags == tag_ref[:, cols], 0.0, big_negative)

    q, k, v = q_ref[...], k_ref[...], v_ref[...]
    grad = nn(g_ref[...], w_ref[...]).astype(BF)
    scores = nt(q, k) * scale + bias_ref[...]
    weights = jnp.exp(scores - jnp.max(scores, axis=1, keepdims=True))
    probs = weights * (1.0 / jnp.sum(weights, axis=1, keepdims=True))
    low = probs.astype(BF)
    attended = nn(low, v).astype(BF)
    delta = jnp.sum(grad.astype(F32) * attended.astype(F32), axis=1, keepdims=True)
    grad_scores = (probs * (nt(grad, v) - delta) * scale).astype(BF)
    att_ref[...] = attended
    for m, part in enumerate((nn(grad_scores, k), tn(grad_scores, q), tn(low, grad))):
        ret_ref[:, m * HEAD_DIM : (m + 1) * HEAD_DIM] = part.astype(BF)


def flip(in_ref, out_ref):
    out_ref[...] = jnp.transpose(in_ref[...].astype(F32)).astype(BF)


def unpack(back_ref, ret_ref, *outs):
    rows_out = nn(back_ref[...], ret_ref[...]).astype(BF)
    for h in range(UNIT // HEAD_DIM):
        for m, ref in enumerate(outs):
            cols = slice(h * HEAD_DIM, (h + 1) * HEAD_DIM)
            base = (h * len(outs) + m) * HEAD_DIM
            ref[:, cols] = rows_out[:, base : base + HEAD_DIM]


def finish(factor, nx, at_ref, *refs):
    ins, out_ref = refs[:-1], refs[-1]
    total = ins[0][...].astype(F32)
    for ref in ins[1:]:
        total = total + ref[...].astype(F32)
    total = total * factor
    share = total.shape[1] // nx
    for s in range(nx):
        source = at_ref[0] ^ (s ^ (s >> 1))
        cols = pl.ds(pl.multiple_of(source * share, share), share)
        out_ref[:, cols] = total[:, s * share : (s + 1) * share]


def cost(flops, nbytes, exps=0):
    return pl.CostEstimate(flops=flops, bytes_accessed=nbytes, transcendentals=exps)


def params():
    return pltpu.CompilerParams(vmem_limit_bytes=67043328)


def ring(size, shift):
    return [(i, (i + shift) % size) for i in range(size)]


def local(sizes, queries, keys, values, grad_out, w_out, cluster_id):
    ny, nz, nc, nx = sizes
    node_count = ny * nz * nc
    rows = queries.shape[1]
    width = queries.shape[2]
    bucket = rows // node_count
    units = width // UNIT
    ua, ub = UNITS_A, units - UNITS_A
    scale = 1.0 / math.sqrt(HEAD_DIM)
    norm_factor = 1.0 / math.sqrt(nx * node_count * rows)
    q, k, v, g = queries[0], keys[0], values[0], grad_out[0]

    def sds(shape, dtype=BF):
        return jax.ShapeDtypeStruct(shape, dtype)

    def full(shape):
        return pl.BlockSpec(shape, lambda *_: (0,) * len(shape))

    def exchange(rows_in):
        c = rows_in.shape[1]
        out = lax.all_to_all(
            rows_in.reshape(node_count, bucket, c),
            "nodes",
            split_axis=0,
            concat_axis=0,
            tiled=True,
        )
        return out.reshape(rows, c)

    wide_a = width + 3 * UNIT * ua
    part_a = pl.BlockSpec((rows, UNIT * ua), lambda i: (0, 0))
    send_a, pick, tags = pl.pallas_call(
        lambda *refs: pack_first(rows, bucket, *refs),
        out_shape=(sds((rows, wide_a)), sds((rows, rows)), sds((1, rows))),
        grid=(1,),
        in_specs=[full((1, rows)), full((rows, width)), part_a, part_a, part_a],
        out_specs=(full((rows, wide_a)), full((rows, rows)), full((1, rows))),
        compiler_params=params(),
        cost_estimate=cost(2 * rows * rows * wide_a, 4 * rows * wide_a),
        name="pack_first",
    )(cluster_id, g, q, k, v)
    recv_a = exchange(send_a)

    node = lax.axis_index("nodes")
    ix = lax.axis_index("rep")
    iy, iz, ic = node // (nz * nc), (node // nc) % nz, node % nc

    def nid(y, z, c):
        return ((y % ny) * nz + z % nz) * nc + c % nc

    everyone = [(y, z, c) for y in range(ny) for z in range(nz) for c in range(nc)]

    def hop(dy, dz, dc):
        return [(nid(y, z, c), nid(y + dy, z + dz, c + dc)) for y, z, c in everyone]

    def pick_of(array, index, axis):
        return lax.dynamic_index_in_dim(array, index, axis, keepdims=False)

    def around(line, count, step):
        return [line] + [lax.ppermute(line, "nodes", hop(*step(s))) for s in range(1, count)]

    line = jnp.concatenate(around(tags, nc, lambda s: (0, 0, s)), axis=0)
    step = 1
    while step < ny:
        line = jnp.concatenate([line, lax.ppermute(line, "nodes", hop(step, 0, 0))], axis=0)
        step *= 2
    lines = around(line, nz, lambda s: (0, s, 0))
    tag_line = pl.pallas_call(
        lambda *refs: tag_order((ny, nz, nc), bucket, *refs),
        out_shape=sds((1, rows), F32),
        in_specs=[pl.BlockSpec(memory_space=pltpu.SMEM)]
        + [pl.BlockSpec(memory_space=pltpu.VMEM)] * nz,
        cost_estimate=cost(2 * rows * rows * LANES, 4 * rows * rows),
        name="tag_order",
    )(jnp.stack([iy, iz, ic]), *lines)

    part_b = pl.BlockSpec((rows, UNIT), lambda i: (0, i + ua))
    send_b = pl.pallas_call(
        pack_rest,
        out_shape=sds((rows, 3 * UNIT * ub)),
        grid=(ub,),
        in_specs=[full((rows, rows)), part_b, part_b, part_b],
        out_specs=pl.BlockSpec((rows, 3 * UNIT), lambda i: (0, i)),
        compiler_params=params(),
        cost_estimate=cost(2 * rows * rows * 3 * UNIT * ub, 4 * rows * 3 * UNIT * ub),
        name="pack_rest",
    )(pick, q, k, v)
    recv_b = exchange(send_b)

    per = UNIT // HEAD_DIM

    def attention(recv, first, unit0, n_units, made):
        def col(m):
            return pl.BlockSpec(
                (rows, HEAD_DIM), lambda i: (0, per * (first + 3 * (i // per) + m) + i % per)
            )

        return pl.pallas_call(
            lambda *refs: attend(scale, *refs),
            out_shape=(sds((rows, 3 * width)), sds((rows, width))),
            grid=(n_units * per,),
            in_specs=[
                full((rows, width)),
                full((1, rows)),
                pl.BlockSpec((width, HEAD_DIM), lambda i: (0, i + unit0 * per)),
                col(0),
                col(1),
                col(2),
            ]
            + [pl.BlockSpec(memory_space=pl.ANY)] * len(made),
            out_specs=(
                pl.BlockSpec((rows, 3 * HEAD_DIM), lambda i: (0, i + unit0 * per)),
                pl.BlockSpec((rows, HEAD_DIM), lambda i: (0, i + unit0 * per)),
            ),
            scratch_shapes=[pltpu.VMEM((rows, rows), F32)],
            input_output_aliases={6 + m: m for m in range(len(made))},
            compiler_params=params(),
            cost_estimate=cost(
                2 * rows * UNIT * n_units * (6 * rows + width),
                2 * rows * UNIT * n_units * 7 + 4 * rows * width,
                rows * rows * n_units * UNIT // HEAD_DIM,
            ),
            name="attend",
        )(recv_a, tag_line, w_out, recv, recv, recv, *made)

    made = attention(recv_a, width // UNIT, 0, ua, ())
    ret, att = attention(recv_b, 0, ua, ub, made)
    home = exchange(ret)
    turned = pl.pallas_call(
        flip,
        out_shape=sds((rows, rows)),
        compiler_params=params(),
        cost_estimate=cost(0, 4 * rows * rows),
        name="flip",
    )(pick)
    outs = pl.pallas_call(
        unpack,
        out_shape=(sds((rows, width)),) * 3,
        grid=(units,),
        in_specs=[full((rows, rows)), pl.BlockSpec((rows, 3 * UNIT), lambda i: (0, i))],
        out_specs=(pl.BlockSpec((rows, UNIT), lambda i: (0, i)),) * 3,
        compiler_params=params(),
        cost_estimate=cost(2 * rows * rows * 3 * width, 12 * rows * width),
        name="unpack",
    )(turned, home)

    share = width // nx

    weight = tn(recv_a[:, :width], att)
    weight = weight.reshape(ny * nz, nc, width // node_count, width)
    total = pick_of(weight, ic, 1)
    for s in range(1, nc):
        sent = pick_of(weight, (ic + s) % nc, 1).astype(BF)
        came = lax.ppermute(sent, "nodes", hop(0, 0, s))
        total = total + came
    weight = total.reshape(width // nc, width)
    came = []
    for s in range(1, nx):
        sent = lax.dynamic_slice_in_dim(weight, ((ix + s) % nx) * share, share, 1).astype(BF)
        came.append(lax.ppermute(sent, "rep", ring(nx, s)))
    total = lax.dynamic_slice_in_dim(weight, ix * share, share, 1)
    for piece in came:
        total = total + piece
    weight = lax.optimization_barrier(total)
    weight = weight.reshape(ny, width // nc // ny, share)
    came = []
    for s in range(1, ny):
        sent = pick_of(weight, (iy + s) % ny, 0).astype(BF)
        came.append(lax.ppermute(sent, "nodes", hop(s, 0, 0)))
    total = pick_of(weight, iy, 0)
    for piece in came:
        total = total + piece
    low = lax.optimization_barrier(total).astype(BF)
    held, turn = 1, low
    while held < nx:
        mask = 2 * held - 1
        came = lax.ppermute(turn, "rep", [(i, i ^ mask) for i in range(nx)])
        turn = jnp.concatenate([turn, came], axis=1)
        held *= 2
    weight = lax.optimization_barrier(turn)
    weight = weight.reshape(nz, width // node_count, width)
    shares = [pick_of(weight, iz, 0)]
    for s in range(1, nz):
        sent = pick_of(weight, (iz + s) % nz, 0)
        shares.append(lax.ppermute(sent, "nodes", hop(0, s, 0)))
    grad_weight = pl.pallas_call(
        lambda *refs: finish(norm_factor, nx, *refs),
        out_shape=sds((width // node_count, width), F32),
        in_specs=[pl.BlockSpec(memory_space=pltpu.SMEM)]
        + [pl.BlockSpec(memory_space=pltpu.VMEM)] * nz,
        cost_estimate=cost(0, 6 * width // node_count * width),
        name="finish",
    )(ix.reshape(1), *shares)
    return (outs[0][None], outs[1][None], outs[2][None], grad_weight)


def solution(mesh):
    nodes, nx = mesh.shape["nodes"], mesh.shape["rep"]
    nc = 2
    nz = 8
    ny = nodes // (nz * nc)
    in_specs = (
        P("rep", "nodes", None),
        P("rep", "nodes", None),
        P("rep", "nodes", None),
        P("rep", "nodes", None),
        P(),
        P("rep", "nodes"),
    )
    out_specs = (
        P("rep", "nodes", None),
        P("rep", "nodes", None),
        P("rep", "nodes", None),
        P("nodes", None),
    )

    def body(*args):
        return local((ny, nz, nc, nx), *args)

    return jax.shard_map(
        body, mesh=mesh, in_specs=in_specs, out_specs=out_specs, check_vma=False
    )
```

```python
import math

import jax
import jax.numpy as jnp
from jax import lax
from jax.experimental import pallas as pl
from jax.experimental.pallas import tpu as pltpu
from jax.sharding import PartitionSpec as P


HEAD_DIM = 128
CL_DEV = 4
UNIT = 256
UNITS_A = 3
LANES = 128
TAG_ROWS = 16
big_negative = -1e30
BF = jnp.bfloat16
F32 = jnp.float32


def mm(a, b, dims):
    return lax.dot_general(a, b, (dims, ((), ())), preferred_element_type=F32)


def nn(a, b):
    return mm(a, b, ((1,), (0,)))


def nt(a, b):
    return mm(a, b, ((1,), (1,)))


def tn(a, b):
    return mm(a, b, ((0,), (0,)))


def column_of(row, rows):
    return jnp.transpose(jnp.broadcast_to(row, (LANES, rows)))[:, :1]


def pack_first(rows, bucket, ids_ref, g_ref, q_ref, k_ref, v_ref, out_ref, pick_ref, tag_ref):
    ids_row = ids_ref[...].astype(F32)
    owner_row = jnp.floor(ids_row * (1.0 / CL_DEV))
    ids_col = column_of(ids_row, rows)
    owner_col = jnp.floor(ids_col * (1.0 / CL_DEV))
    tag_row = ids_row - owner_row * CL_DEV + 1.0
    down = lax.broadcasted_iota(jnp.int32, (rows, rows), 0)
    across = lax.broadcasted_iota(jnp.int32, (rows, rows), 1)
    same = (owner_col == owner_row) & (down < across)
    rank = jnp.sum(jnp.where(same, 1.0, 0.0), axis=0, keepdims=True)
    slot = (owner_row * bucket + rank).astype(jnp.int32)
    pick = jnp.where(down == slot, 1.0, 0.0).astype(BF)
    pick_ref[...] = pick
    tags = jnp.broadcast_to(tag_row, (TAG_ROWS, rows)).astype(BF)
    tag_ref[...] = nt(tags, pick)[:1].astype(BF)
    width = g_ref.shape[1]
    out_ref[:, :width] = nn(pick, g_ref[...]).astype(BF)
    for u in range(q_ref.shape[1] // UNIT):
        for m, ref in enumerate((q_ref, k_ref, v_ref)):
            base = width + (3 * u + m) * UNIT
            out_ref[:, base : base + UNIT] = nn(pick, ref[:, u * UNIT : (u + 1) * UNIT]).astype(BF)


def tag_order(sizes, bucket, at_ref, *refs):
    ny, nz, nc = sizes
    nodes = ny * nz * nc
    ins, out_ref = refs[:-1], refs[-1]
    iy, iz, ic = at_ref[0], at_ref[1], at_ref[2]
    table = jnp.concatenate([ref[...].astype(F32) for ref in ins], axis=0)
    rows = table.shape[1]
    lane = lax.broadcasted_iota(jnp.int32, (rows, LANES), 0)
    k = lax.broadcasted_iota(jnp.int32, (rows, LANES), 1)
    me = (iy * nz + iz) * nc + ic
    mine = jnp.where((lane == me * bucket + k) & (k < bucket), 1.0, 0.0).astype(BF)
    table = nn(table.astype(BF), mine)
    n = lax.broadcasted_iota(jnp.int32, (nodes, nodes), 0)
    at = lax.broadcasted_iota(jnp.int32, (nodes, nodes), 1)
    bits_c, bits_z = nc.bit_length() - 1, nz.bit_length() - 1
    dc = (ic - n) & (nc - 1)
    dz = (iz - (n >> bits_c)) & (nz - 1)
    dy = (iy - (n >> (bits_c + bits_z))) & (ny - 1)
    turn = jnp.where(at == (dz * ny + dy) * nc + dc, 1.0, 0.0).astype(BF)
    table = nn(turn, table.astype(BF)).astype(BF)
    n = lax.broadcasted_iota(jnp.int32, (nodes, rows), 0)
    slot = lax.broadcasted_iota(jnp.int32, (nodes, rows), 1)
    bits_k = bucket.bit_length() - 1
    spread = tn(table, jnp.where((slot >> bits_k) == n, 1.0, 0.0).astype(BF))
    k = lax.broadcasted_iota(jnp.int32, spread.shape, 0)
    slot = lax.broadcasted_iota(jnp.int32, spread.shape, 1)
    kept = jnp.where((slot & (bucket - 1)) == k, spread, 0.0)
    out_ref[...] = jnp.sum(kept, axis=0, keepdims=True)


def pack_rest(pick_ref, q_ref, k_ref, v_ref, out_ref):
    pick = pick_ref[...]
    for m, ref in enumerate((q_ref, k_ref, v_ref)):
        out_ref[:, m * UNIT : (m + 1) * UNIT] = nn(pick, ref[...]).astype(BF)


def attend(scale, tag_ref, grad_ref, q_ref, k_ref, v_ref, *refs):
    ret_ref, att_ref, bias_ref = refs[-3:]
    rows = q_ref.shape[0]

    @pl.when(pl.program_id(0) == 0)
    def _():
        tags = column_of(tag_ref[...], rows)

        @pl.loop(0, rows // LANES)
        def _(j):
            cols = pl.ds(pl.multiple_of(j * LANES, LANES), LANES)
            bias_ref[:, cols] = jnp.where(tags == tag_ref[:, cols], 0.0, big_negative)

    for h in range(UNIT // HEAD_DIM):
        cols = slice(h * HEAD_DIM, (h + 1) * HEAD_DIM)
        q, k, v, grad = q_ref[:, cols], k_ref[:, cols], v_ref[:, cols], grad_ref[:, cols]
        scores = nt(q, k) * scale + bias_ref[...]
        weights = jnp.exp(scores - jnp.max(scores, axis=1, keepdims=True))
        probs = weights * (1.0 / jnp.sum(weights, axis=1, keepdims=True))
        low = probs.astype(BF)
        attended = nn(low, v).astype(BF)
        delta = jnp.sum(grad.astype(F32) * attended.astype(F32), axis=1, keepdims=True)
        grad_scores = (probs * (nt(grad, v) - delta) * scale).astype(BF)
        att_ref[:, cols] = attended
        for m, part in enumerate((nn(grad_scores, k), tn(grad_scores, q), tn(low, grad))):
            base = m * UNIT + h * HEAD_DIM
            ret_ref[:, base : base + HEAD_DIM] = part.astype(BF)


def flip(in_ref, out_ref):
    out_ref[...] = jnp.transpose(in_ref[...].astype(F32)).astype(BF)


def unpack(back_ref, ret_ref, *outs):
    for m, ref in enumerate(outs):
        ref[...] = nn(back_ref[...], ret_ref[:, m * UNIT : (m + 1) * UNIT]).astype(BF)


def finish(factor, nx, at_ref, *refs):
    ins, out_ref = refs[:-1], refs[-1]
    total = ins[0][...].astype(F32)
    for ref in ins[1:]:
        total = total + ref[...].astype(F32)
    total = total * factor
    share = total.shape[1] // nx
    for s in range(nx):
        source = at_ref[0] ^ (s ^ (s >> 1))
        cols = pl.ds(pl.multiple_of(source * share, share), share)
        out_ref[:, cols] = total[:, s * share : (s + 1) * share]


def cost(flops, nbytes, exps=0):
    return pl.CostEstimate(flops=flops, bytes_accessed=nbytes, transcendentals=exps)


def params():
    return pltpu.CompilerParams(vmem_limit_bytes=67043328)


def ring(size, shift):
    return [(i, (i + shift) % size) for i in range(size)]


def local(sizes, queries, keys, values, grad_out, w_out, cluster_id):
    ny, nz, nc, nx = sizes
    node_count = ny * nz * nc
    rows = queries.shape[1]
    width = queries.shape[2]
    bucket = rows // node_count
    units = width // UNIT
    ua, ub = UNITS_A, units - UNITS_A
    scale = 1.0 / math.sqrt(HEAD_DIM)
    norm_factor = 1.0 / math.sqrt(nx * node_count * rows)
    q, k, v, g = queries[0], keys[0], values[0], grad_out[0]

    def sds(shape, dtype=BF):
        return jax.ShapeDtypeStruct(shape, dtype)

    def full(shape):
        return pl.BlockSpec(shape, lambda *_: (0,) * len(shape))

    def exchange(rows_in):
        c = rows_in.shape[1]
        out = lax.all_to_all(
            rows_in.reshape(node_count, bucket, c),
            "nodes",
            split_axis=0,
            concat_axis=0,
            tiled=True,
        )
        return out.reshape(rows, c)

    wide_a = width + 3 * UNIT * ua
    part_a = pl.BlockSpec((rows, UNIT * ua), lambda i: (0, 0))
    send_a, pick, tags = pl.pallas_call(
        lambda *refs: pack_first(rows, bucket, *refs),
        out_shape=(sds((rows, wide_a)), sds((rows, rows)), sds((1, rows))),
        grid=(1,),
        in_specs=[full((1, rows)), full((rows, width)), part_a, part_a, part_a],
        out_specs=(full((rows, wide_a)), full((rows, rows)), full((1, rows))),
        compiler_params=params(),
        cost_estimate=cost(2 * rows * rows * wide_a, 4 * rows * wide_a),
        name="pack_first",
    )(cluster_id, g, q, k, v)
    recv_a = exchange(send_a)

    node = lax.axis_index("nodes")
    ix = lax.axis_index("rep")
    iy, iz, ic = node // (nz * nc), (node // nc) % nz, node % nc

    def nid(y, z, c):
        return ((y % ny) * nz + z % nz) * nc + c % nc

    everyone = [(y, z, c) for y in range(ny) for z in range(nz) for c in range(nc)]

    def hop(dy, dz, dc):
        return [(nid(y, z, c), nid(y + dy, z + dz, c + dc)) for y, z, c in everyone]

    def pick_of(array, index, axis):
        return lax.dynamic_index_in_dim(array, index, axis, keepdims=False)

    def around(line, count, step):
        return [line] + [lax.ppermute(line, "nodes", hop(*step(s))) for s in range(1, count)]

    line = jnp.concatenate(around(tags, nc, lambda s: (0, 0, s)), axis=0)
    step = 1
    while step < ny:
        line = jnp.concatenate([line, lax.ppermute(line, "nodes", hop(step, 0, 0))], axis=0)
        step *= 2
    lines = around(line, nz, lambda s: (0, s, 0))
    tag_line = pl.pallas_call(
        lambda *refs: tag_order((ny, nz, nc), bucket, *refs),
        out_shape=sds((1, rows), F32),
        in_specs=[pl.BlockSpec(memory_space=pltpu.SMEM)]
        + [pl.BlockSpec(memory_space=pltpu.VMEM)] * nz,
        cost_estimate=cost(2 * rows * rows * LANES, 4 * rows * rows),
        name="tag_order",
    )(jnp.stack([iy, iz, ic]), *lines)

    part_b = pl.BlockSpec((rows, UNIT), lambda i: (0, i + ua))
    send_b = pl.pallas_call(
        pack_rest,
        out_shape=sds((rows, 3 * UNIT * ub)),
        grid=(ub,),
        in_specs=[full((rows, rows)), part_b, part_b, part_b],
        out_specs=pl.BlockSpec((rows, 3 * UNIT), lambda i: (0, i)),
        compiler_params=params(),
        cost_estimate=cost(2 * rows * rows * 3 * UNIT * ub, 4 * rows * 3 * UNIT * ub),
        name="pack_rest",
    )(pick, q, k, v)
    recv_b = exchange(send_b)

    grad_attended = nn(recv_a[:, :width], w_out).astype(BF)

    def attention(recv, first, unit0, n_units, made):
        def col(m):
            return pl.BlockSpec((rows, UNIT), lambda i: (0, first + 3 * i + m))

        return pl.pallas_call(
            lambda *refs: attend(scale, *refs),
            out_shape=(sds((rows, 3 * width)), sds((rows, width))),
            grid=(n_units,),
            in_specs=[
                full((1, rows)),
                pl.BlockSpec((rows, UNIT), lambda i: (0, i + unit0)),
                col(0),
                col(1),
                col(2),
            ]
            + [pl.BlockSpec(memory_space=pl.ANY)] * len(made),
            out_specs=(
                pl.BlockSpec((rows, 3 * UNIT), lambda i: (0, i + unit0)),
                pl.BlockSpec((rows, UNIT), lambda i: (0, i + unit0)),
            ),
            scratch_shapes=[pltpu.VMEM((rows, rows), F32)],
            input_output_aliases={5 + m: m for m in range(len(made))},
            compiler_params=params(),
            cost_estimate=cost(
                2 * rows * UNIT * n_units * 6 * rows,
                2 * rows * UNIT * n_units * 8,
                rows * rows * n_units * UNIT // HEAD_DIM,
            ),
            name="attend",
        )(tag_line, grad_attended, recv, recv, recv, *made)

    made = attention(recv_a, width // UNIT, 0, ua, ())
    ret, att = attention(recv_b, 0, ua, ub, made)
    home = exchange(ret)
    turned = pl.pallas_call(
        flip,
        out_shape=sds((rows, rows)),
        compiler_params=params(),
        cost_estimate=cost(0, 4 * rows * rows),
        name="flip",
    )(pick)
    outs = pl.pallas_call(
        unpack,
        out_shape=(sds((rows, width)),) * 3,
        grid=(units,),
        in_specs=[full((rows, rows)), pl.BlockSpec((rows, 3 * UNIT), lambda i: (0, i))],
        out_specs=(pl.BlockSpec((rows, UNIT), lambda i: (0, i)),) * 3,
        compiler_params=params(),
        cost_estimate=cost(2 * rows * rows * 3 * width, 12 * rows * width),
        name="unpack",
    )(turned, home)

    share = width // nx

    weight = tn(recv_a[:, :width], att)
    weight = weight.reshape(ny * nz, nc, width // node_count, width)
    total = pick_of(weight, ic, 1)
    for s in range(1, nc):
        sent = pick_of(weight, (ic + s) % nc, 1).astype(BF)
        came = lax.ppermute(sent, "nodes", hop(0, 0, s))
        total = total + came
    weight = total.reshape(width // nc, width)
    came = []
    for s in range(1, nx):
        sent = lax.dynamic_slice_in_dim(weight, ((ix + s) % nx) * share, share, 1).astype(BF)
        came.append(lax.ppermute(sent, "rep", ring(nx, s)))
    total = lax.dynamic_slice_in_dim(weight, ix * share, share, 1)
    for piece in came:
        total = total + piece
    weight = lax.optimization_barrier(total)
    weight = weight.reshape(ny, width // nc // ny, share)
    came = []
    for s in range(1, ny):
        sent = pick_of(weight, (iy + s) % ny, 0).astype(BF)
        came.append(lax.ppermute(sent, "nodes", hop(s, 0, 0)))
    total = pick_of(weight, iy, 0)
    for piece in came:
        total = total + piece
    low = lax.optimization_barrier(total).astype(BF)
    held, turn = 1, low
    while held < nx:
        mask = 2 * held - 1
        came = lax.ppermute(turn, "rep", [(i, i ^ mask) for i in range(nx)])
        turn = jnp.concatenate([turn, came], axis=1)
        held *= 2
    weight = lax.optimization_barrier(turn)
    weight = weight.reshape(nz, width // node_count, width)
    shares = [pick_of(weight, iz, 0)]
    for s in range(1, nz):
        sent = pick_of(weight, (iz + s) % nz, 0)
        shares.append(lax.ppermute(sent, "nodes", hop(0, s, 0)))
    grad_weight = pl.pallas_call(
        lambda *refs: finish(norm_factor, nx, *refs),
        out_shape=sds((width // node_count, width), F32),
        in_specs=[pl.BlockSpec(memory_space=pltpu.SMEM)]
        + [pl.BlockSpec(memory_space=pltpu.VMEM)] * nz,
        cost_estimate=cost(0, 6 * width // node_count * width),
        name="finish",
    )(ix.reshape(1), *shares)
    return (outs[0][None], outs[1][None], outs[2][None], grad_weight)


def solution(mesh):
    nodes, nx = mesh.shape["nodes"], mesh.shape["rep"]
    nc = 2
    nz = 8
    ny = nodes // (nz * nc)
    in_specs = (
        P("rep", "nodes", None),
        P("rep", "nodes", None),
        P("rep", "nodes", None),
        P("rep", "nodes", None),
        P(),
        P("rep", "nodes"),
    )
    out_specs = (
        P("rep", "nodes", None),
        P("rep", "nodes", None),
        P("rep", "nodes", None),
        P("nodes", None),
    )

    def body(*args):
        return local((ny, nz, nc, nx), *args)

    return jax.shard_map(
        body, mesh=mesh, in_specs=in_specs, out_specs=out_specs, check_vma=False
    )
```

```python
import math

import jax
import jax.numpy as jnp
from jax import lax
from jax.experimental import pallas as pl
from jax.experimental.pallas import tpu as pltpu
from jax.sharding import PartitionSpec as P


HEAD_DIM = 128
CL_DEV = 4
UNIT = 256
UNITS_A = 3
LANES = 128
TAG_ROWS = 16
big_negative = -1e30
BF = jnp.bfloat16
F32 = jnp.float32


def mm(a, b, dims):
    return lax.dot_general(a, b, (dims, ((), ())), preferred_element_type=F32)


def nn(a, b):
    return mm(a, b, ((1,), (0,)))


def nt(a, b):
    return mm(a, b, ((1,), (1,)))


def tn(a, b):
    return mm(a, b, ((0,), (0,)))


def column_of(row, rows):
    return jnp.transpose(jnp.broadcast_to(row, (LANES, rows)))[:, :1]


def pack_first(rows, bucket, ids_ref, g_ref, q_ref, k_ref, v_ref, out_ref, pick_ref, tag_ref):
    ids_row = ids_ref[...].astype(F32)
    owner_row = jnp.floor(ids_row * (1.0 / CL_DEV))
    ids_col = column_of(ids_row, rows)
    owner_col = jnp.floor(ids_col * (1.0 / CL_DEV))
    tag_row = ids_row - owner_row * CL_DEV + 1.0
    down = lax.broadcasted_iota(jnp.int32, (rows, rows), 0)
    across = lax.broadcasted_iota(jnp.int32, (rows, rows), 1)
    same = (owner_col == owner_row) & (down < across)
    rank = jnp.sum(jnp.where(same, 1.0, 0.0), axis=0, keepdims=True)
    slot = (owner_row * bucket + rank).astype(jnp.int32)
    pick = jnp.where(down == slot, 1.0, 0.0).astype(BF)
    pick_ref[...] = pick
    tags = jnp.broadcast_to(tag_row, (TAG_ROWS, rows)).astype(BF)
    tag_ref[...] = nt(tags, pick)[:1].astype(BF)
    width = g_ref.shape[1]
    out_ref[:, :width] = nn(pick, g_ref[...]).astype(BF)
    for u in range(q_ref.shape[1] // UNIT):
        for m, ref in enumerate((q_ref, k_ref, v_ref)):
            base = width + (3 * u + m) * UNIT
            out_ref[:, base : base + UNIT] = nn(pick, ref[:, u * UNIT : (u + 1) * UNIT]).astype(BF)


def tag_order(sizes, bucket, at_ref, *refs):
    ny, nz, nc = sizes
    nodes = ny * nz * nc
    ins, out_ref = refs[:-1], refs[-1]
    iy, iz, ic = at_ref[0], at_ref[1], at_ref[2]
    table = jnp.concatenate([ref[...].astype(F32) for ref in ins], axis=0)
    rows = table.shape[1]
    lane = lax.broadcasted_iota(jnp.int32, (rows, LANES), 0)
    k = lax.broadcasted_iota(jnp.int32, (rows, LANES), 1)
    me = (iy * nz + iz) * nc + ic
    mine = jnp.where((lane == me * bucket + k) & (k < bucket), 1.0, 0.0).astype(BF)
    table = nn(table.astype(BF), mine)
    n = lax.broadcasted_iota(jnp.int32, (nodes, nodes), 0)
    at = lax.broadcasted_iota(jnp.int32, (nodes, nodes), 1)
    bits_c, bits_z = nc.bit_length() - 1, nz.bit_length() - 1
    dc = (ic - n) & (nc - 1)
    dz = (iz - (n >> bits_c)) & (nz - 1)
    dy = (iy - (n >> (bits_c + bits_z))) & (ny - 1)
    turn = jnp.where(at == (dz * ny + dy) * nc + dc, 1.0, 0.0).astype(BF)
    table = nn(turn, table.astype(BF)).astype(BF)
    n = lax.broadcasted_iota(jnp.int32, (nodes, rows), 0)
    slot = lax.broadcasted_iota(jnp.int32, (nodes, rows), 1)
    bits_k = bucket.bit_length() - 1
    spread = tn(table, jnp.where((slot >> bits_k) == n, 1.0, 0.0).astype(BF))
    k = lax.broadcasted_iota(jnp.int32, spread.shape, 0)
    slot = lax.broadcasted_iota(jnp.int32, spread.shape, 1)
    kept = jnp.where((slot & (bucket - 1)) == k, spread, 0.0)
    out_ref[...] = jnp.sum(kept, axis=0, keepdims=True)


def pack_rest(pick_ref, q_ref, k_ref, v_ref, out_ref):
    pick = pick_ref[...]
    for m, ref in enumerate((q_ref, k_ref, v_ref)):
        out_ref[:, m * UNIT : (m + 1) * UNIT] = nn(pick, ref[...]).astype(BF)


def attend(scale, tag_ref, grad_ref, q_ref, k_ref, v_ref, *refs):
    ret_ref, att_ref, bias_ref = refs[-3:]
    rows = q_ref.shape[0]

    @pl.when(pl.program_id(0) == 0)
    def _():
        tags = tag_ref[...]
        bias_ref[...] = jnp.where(column_of(tags, rows) == tags, 0.0, big_negative)

    for h in range(UNIT // HEAD_DIM):
        cols = slice(h * HEAD_DIM, (h + 1) * HEAD_DIM)
        q, k, v, grad = q_ref[:, cols], k_ref[:, cols], v_ref[:, cols], grad_ref[:, cols]
        scores = nt(q, k) * scale + bias_ref[...]
        weights = jnp.exp(scores - jnp.max(scores, axis=1, keepdims=True))
        probs = weights * (1.0 / jnp.sum(weights, axis=1, keepdims=True))
        low = probs.astype(BF)
        attended = nn(low, v).astype(BF)
        delta = jnp.sum(grad.astype(F32) * attended.astype(F32), axis=1, keepdims=True)
        grad_scores = (probs * (nt(grad, v) - delta) * scale).astype(BF)
        att_ref[:, cols] = attended
        for m, part in enumerate((nn(grad_scores, k), tn(grad_scores, q), tn(low, grad))):
            base = m * UNIT + h * HEAD_DIM
            ret_ref[:, base : base + HEAD_DIM] = part.astype(BF)


def flip(in_ref, out_ref):
    out_ref[...] = jnp.transpose(in_ref[...].astype(F32)).astype(BF)


def unpack(back_ref, ret_ref, *outs):
    for m, ref in enumerate(outs):
        ref[...] = nn(back_ref[...], ret_ref[:, m * UNIT : (m + 1) * UNIT]).astype(BF)


def finish(factor, nx, at_ref, *refs):
    ins, out_ref = refs[:-1], refs[-1]
    total = ins[0][...].astype(F32)
    for ref in ins[1:]:
        total = total + ref[...].astype(F32)
    total = total * factor
    share = total.shape[1] // nx
    for s in range(nx):
        source = at_ref[0] ^ (s ^ (s >> 1))
        cols = pl.ds(pl.multiple_of(source * share, share), share)
        out_ref[:, cols] = total[:, s * share : (s + 1) * share]


def cost(flops, nbytes, exps=0):
    return pl.CostEstimate(flops=flops, bytes_accessed=nbytes, transcendentals=exps)


def params():
    return pltpu.CompilerParams(vmem_limit_bytes=67043328)


def ring(size, shift):
    return [(i, (i + shift) % size) for i in range(size)]


def local(sizes, queries, keys, values, grad_out, w_out, cluster_id):
    ny, nz, nc, nx = sizes
    node_count = ny * nz * nc
    rows = queries.shape[1]
    width = queries.shape[2]
    bucket = rows // node_count
    units = width // UNIT
    ua, ub = UNITS_A, units - UNITS_A
    scale = 1.0 / math.sqrt(HEAD_DIM)
    norm_factor = 1.0 / math.sqrt(nx * node_count * rows)
    q, k, v, g = queries[0], keys[0], values[0], grad_out[0]

    def sds(shape, dtype=BF):
        return jax.ShapeDtypeStruct(shape, dtype)

    def full(shape):
        return pl.BlockSpec(shape, lambda *_: (0,) * len(shape))

    def exchange(rows_in):
        c = rows_in.shape[1]
        out = lax.all_to_all(
            rows_in.reshape(node_count, bucket, c),
            "nodes",
            split_axis=0,
            concat_axis=0,
            tiled=True,
        )
        return out.reshape(rows, c)

    wide_a = width + 3 * UNIT * ua
    part_a = pl.BlockSpec((rows, UNIT * ua), lambda i: (0, 0))
    send_a, pick, tags = pl.pallas_call(
        lambda *refs: pack_first(rows, bucket, *refs),
        out_shape=(sds((rows, wide_a)), sds((rows, rows)), sds((1, rows))),
        grid=(1,),
        in_specs=[full((1, rows)), full((rows, width)), part_a, part_a, part_a],
        out_specs=(full((rows, wide_a)), full((rows, rows)), full((1, rows))),
        compiler_params=params(),
        cost_estimate=cost(2 * rows * rows * wide_a, 4 * rows * wide_a),
        name="pack_first",
    )(cluster_id, g, q, k, v)
    recv_a = exchange(send_a)

    node = lax.axis_index("nodes")
    ix = lax.axis_index("rep")
    iy, iz, ic = node // (nz * nc), (node // nc) % nz, node % nc

    def nid(y, z, c):
        return ((y % ny) * nz + z % nz) * nc + c % nc

    everyone = [(y, z, c) for y in range(ny) for z in range(nz) for c in range(nc)]

    def hop(dy, dz, dc):
        return [(nid(y, z, c), nid(y + dy, z + dz, c + dc)) for y, z, c in everyone]

    def pick_of(array, index, axis):
        return lax.dynamic_index_in_dim(array, index, axis, keepdims=False)

    def around(line, count, step):
        return [line] + [lax.ppermute(line, "nodes", hop(*step(s))) for s in range(1, count)]

    line = jnp.concatenate(around(tags, nc, lambda s: (0, 0, s)), axis=0)
    step = 1
    while step < ny:
        line = jnp.concatenate([line, lax.ppermute(line, "nodes", hop(step, 0, 0))], axis=0)
        step *= 2
    lines = around(line, nz, lambda s: (0, s, 0))
    tag_line = pl.pallas_call(
        lambda *refs: tag_order((ny, nz, nc), bucket, *refs),
        out_shape=sds((1, rows), F32),
        in_specs=[pl.BlockSpec(memory_space=pltpu.SMEM)]
        + [pl.BlockSpec(memory_space=pltpu.VMEM)] * nz,
        cost_estimate=cost(2 * rows * rows * LANES, 4 * rows * rows),
        name="tag_order",
    )(jnp.stack([iy, iz, ic]), *lines)

    part_b = pl.BlockSpec((rows, UNIT), lambda i: (0, i + ua))
    send_b = pl.pallas_call(
        pack_rest,
        out_shape=sds((rows, 3 * UNIT * ub)),
        grid=(ub,),
        in_specs=[full((rows, rows)), part_b, part_b, part_b],
        out_specs=pl.BlockSpec((rows, 3 * UNIT), lambda i: (0, i)),
        compiler_params=params(),
        cost_estimate=cost(2 * rows * rows * 3 * UNIT * ub, 4 * rows * 3 * UNIT * ub),
        name="pack_rest",
    )(pick, q, k, v)
    recv_b = exchange(send_b)

    grad_attended = nn(recv_a[:, :width], w_out).astype(BF)

    def attention(recv, first, unit0, n_units, made):
        def col(m):
            return pl.BlockSpec((rows, UNIT), lambda i: (0, first + 3 * i + m))

        return pl.pallas_call(
            lambda *refs: attend(scale, *refs),
            out_shape=(sds((rows, 3 * width)), sds((rows, width))),
            grid=(n_units,),
            in_specs=[
                full((1, rows)),
                pl.BlockSpec((rows, UNIT), lambda i: (0, i + unit0)),
                col(0),
                col(1),
                col(2),
            ]
            + [pl.BlockSpec(memory_space=pl.ANY)] * len(made),
            out_specs=(
                pl.BlockSpec((rows, 3 * UNIT), lambda i: (0, i + unit0)),
                pl.BlockSpec((rows, UNIT), lambda i: (0, i + unit0)),
            ),
            scratch_shapes=[pltpu.VMEM((rows, rows), F32)],
            input_output_aliases={5 + m: m for m in range(len(made))},
            compiler_params=params(),
            cost_estimate=cost(
                2 * rows * UNIT * n_units * 6 * rows,
                2 * rows * UNIT * n_units * 8,
                rows * rows * n_units * UNIT // HEAD_DIM,
            ),
            name="attend",
        )(tag_line, grad_attended, recv, recv, recv, *made)

    made = attention(recv_a, width // UNIT, 0, ua, ())
    ret, att = attention(recv_b, 0, ua, ub, made)
    home = exchange(ret)
    turned = pl.pallas_call(
        flip,
        out_shape=sds((rows, rows)),
        compiler_params=params(),
        cost_estimate=cost(0, 4 * rows * rows),
        name="flip",
    )(pick)
    outs = pl.pallas_call(
        unpack,
        out_shape=(sds((rows, width)),) * 3,
        grid=(units,),
        in_specs=[full((rows, rows)), pl.BlockSpec((rows, 3 * UNIT), lambda i: (0, i))],
        out_specs=(pl.BlockSpec((rows, UNIT), lambda i: (0, i)),) * 3,
        compiler_params=params(),
        cost_estimate=cost(2 * rows * rows * 3 * width, 12 * rows * width),
        name="unpack",
    )(turned, home)

    share = width // nx

    weight = tn(recv_a[:, :width], att)
    weight = weight.reshape(ny * nz, nc, width // node_count, width)
    total = pick_of(weight, ic, 1)
    for s in range(1, nc):
        sent = pick_of(weight, (ic + s) % nc, 1).astype(BF)
        came = lax.ppermute(sent, "nodes", hop(0, 0, s))
        total = total + came
    weight = total.reshape(width // nc, width)
    came = []
    for s in range(1, nx):
        sent = lax.dynamic_slice_in_dim(weight, ((ix + s) % nx) * share, share, 1).astype(BF)
        came.append(lax.ppermute(sent, "rep", ring(nx, s)))
    total = lax.dynamic_slice_in_dim(weight, ix * share, share, 1)
    for piece in came:
        total = total + piece
    weight = lax.optimization_barrier(total)
    weight = weight.reshape(ny, width // nc // ny, share)
    came = []
    for s in range(1, ny):
        sent = pick_of(weight, (iy + s) % ny, 0).astype(BF)
        came.append(lax.ppermute(sent, "nodes", hop(s, 0, 0)))
    total = pick_of(weight, iy, 0)
    for piece in came:
        total = total + piece
    low = lax.optimization_barrier(total).astype(BF)
    held, turn = 1, low
    while held < nx:
        mask = 2 * held - 1
        came = lax.ppermute(turn, "rep", [(i, i ^ mask) for i in range(nx)])
        turn = jnp.concatenate([turn, came], axis=1)
        held *= 2
    weight = lax.optimization_barrier(turn)
    weight = weight.reshape(nz, width // node_count, width)
    shares = [pick_of(weight, iz, 0)]
    for s in range(1, nz):
        sent = pick_of(weight, (iz + s) % nz, 0)
        shares.append(lax.ppermute(sent, "nodes", hop(0, s, 0)))
    grad_weight = pl.pallas_call(
        lambda *refs: finish(norm_factor, nx, *refs),
        out_shape=sds((width // node_count, width), F32),
        in_specs=[pl.BlockSpec(memory_space=pltpu.SMEM)]
        + [pl.BlockSpec(memory_space=pltpu.VMEM)] * nz,
        cost_estimate=cost(0, 6 * width // node_count * width),
        name="finish",
    )(ix.reshape(1), *shares)
    return (outs[0][None], outs[1][None], outs[2][None], grad_weight)


def solution(mesh):
    nodes, nx = mesh.shape["nodes"], mesh.shape["rep"]
    nc = 2
    nz = 8
    ny = nodes // (nz * nc)
    in_specs = (
        P("rep", "nodes", None),
        P("rep", "nodes", None),
        P("rep", "nodes", None),
        P("rep", "nodes", None),
        P(),
        P("rep", "nodes"),
    )
    out_specs = (
        P("rep", "nodes", None),
        P("rep", "nodes", None),
        P("rep", "nodes", None),
        P("nodes", None),
    )

    def body(*args):
        return local((ny, nz, nc, nx), *args)

    return jax.shard_map(
        body, mesh=mesh, in_specs=in_specs, out_specs=out_specs, check_vma=False
    )
```
